128 devices in a mesh: blk: 32 (over y_hi, z, x), rep: 4 (over y_lo, core).
Axes of the slice: x: 4, y: 4 (y_hi: 2, y_lo: 2; y = y_hi * 2 + y_lo), z: 4, core: 2. Of those that a mesh axis runs over, the one named last changes fastest.
Arguments:
- image_emb: bfloat16 [16384, 1024], P(('blk', 'rep')), may hold values from -8 to 8
- curve_emb: bfloat16 [16384, 1024], P(('blk', 'rep')), may hold values from -8 to 8
Outputs:
- loss_value: float32 [], replicated
- image_grad: float32 [16384, 1024], P(('blk', 'rep'))
- curve_grad: float32 [16384, 1024], P(('blk', 'rep'))
The draws below stay inside these ranges and needn't reach their ends.
All inputs are finite; a program needn't handle non-finite values.
Results may differ from the reference program's by a relative error of at most 0.0015.
Values may be sent and summed in bfloat16 or wider, within the bound.
A program may use at most 128 MiB of HBM per device.

```python
import math
import jax
import jax.numpy as jnp
from jax import lax

D = 1024
PAIRS = 16384


def make_pair(key):
    base_key = jax.random.fold_in(key, 11)
    key_list = jax.random.split(base_key, 5)
    position = jnp.arange(PAIRS, dtype=jnp.float32) / PAIRS
    root_width = math.sqrt(D)

    def row_scales(sub_key):
        spread = jax.random.uniform(sub_key, (PAIRS,), jnp.float32)
        return jnp.exp(jnp.log(0.3) + jnp.log(10.0) * (0.5 * position + 0.5 * spread))
    image_raw = jax.random.normal(key_list[0], (PAIRS, D), jnp.float32)
    curve_raw = jax.random.normal(key_list[1], (PAIRS, D), jnp.float32)
    image_out = row_scales(key_list[3])[:, None] * image_raw / root_width
    curve_out = row_scales(key_list[4])[:, None] * curve_raw / root_width
    image_out = jnp.clip(image_out, -8.0, 8.0)
    curve_out = jnp.clip(curve_out, -8.0, 8.0)
    return (image_out, curve_out)


def draw_image_emb(key, part):
    return make_pair(key)[0].astype(jnp.bfloat16)


def draw_curve_emb(key, part):
    return make_pair(key)[1].astype(jnp.bfloat16)


def setup_inputs(seed: int = 0) -> dict:
    key_of = jax.random.split(jax.random.key(seed), 3)
    image_emb = draw_image_emb(jax.random.fold_in(key_of[2], 71), 0)
    curve_emb = draw_curve_emb(jax.random.fold_in(key_of[2], 71), 0)
    return dict(image_emb=image_emb, curve_emb=curve_emb)


def reference(image_emb, curve_emb):
    pair_count = image_emb.shape[0]
    logit_gain = math.sqrt(D)
    block_size = min(pair_count, 1024)
    block_count = pair_count // block_size
    image_blocks = image_emb.reshape(block_count, block_size, D)

    def forward_step(carried, image_rows):
        scores = jnp.dot(image_rows, curve_emb.T, preferred_element_type=jnp.float32) * logit_gain
        highest = lax.optimization_barrier(jnp.max(scores, axis=1))
        row_part = highest + jnp.log(lax.optimization_barrier(jnp.sum(jnp.exp(scores - highest[:, None]), axis=1)))
        column_high = jnp.maximum(carried[0], lax.optimization_barrier(jnp.max(scores, axis=0)))
        column_sum = carried[1] * jnp.exp(carried[0] - column_high) + lax.optimization_barrier(jnp.sum(jnp.exp(scores - column_high[None, :]), axis=0))
        return ((column_high, column_sum), row_part)
    initial = (jnp.full((pair_count,), -1e+30, jnp.float32), jnp.zeros((pair_count,), jnp.float32))
    (column_high, column_sum), row_blocks = lax.scan(forward_step, initial, image_blocks)
    row_lse = row_blocks.reshape(pair_count)
    col_lse = column_high + jnp.log(column_sum)
    positive = lax.optimization_barrier(jnp.sum(image_emb.astype(jnp.float32) * curve_emb.astype(jnp.float32), axis=1)) * logit_gain
    loss_value = (jnp.sum(row_lse - positive) + jnp.sum(col_lse - positive)) / (2.0 * pair_count)

    def backward_step(curve_acc, packed):
        image_rows, row_part = packed
        scores = jnp.dot(image_rows, curve_emb.T, preferred_element_type=jnp.float32) * logit_gain
        weight = ((jnp.exp(scores - row_part[:, None]) + jnp.exp(scores - col_lse[None, :])) * 0.5).astype(jnp.bfloat16)
        rows_grad = jnp.dot(weight, curve_emb, preferred_element_type=jnp.float32) * logit_gain
        curve_acc = curve_acc + jnp.dot(weight.T, image_rows, preferred_element_type=jnp.float32) * logit_gain
        return (curve_acc, rows_grad)
    curve_acc, image_parts = lax.scan(backward_step, jnp.zeros((pair_count, D), jnp.float32), (image_blocks, row_lse.reshape(block_count, block_size)))
    image_grad = image_parts.reshape(pair_count, D) - logit_gain * curve_emb.astype(jnp.float32)
    curve_grad = curve_acc - logit_gain * image_emb.astype(jnp.float32)
    return (loss_value, image_grad, curve_grad)
```

```python
import functools
import math

import jax
import jax.numpy as jnp
from jax import lax
from jax.experimental import pallas as pl
from jax.experimental.pallas import tpu as pltpu
from jax.sharding import PartitionSpec as P

F32, BF16 = jnp.float32, jnp.bfloat16
MESH = pl.DeviceIdType.MESH
HOPS = (2, 1, 3)


def nt(a, b):
    return lax.dot_general(a, b, (((1,), (1,)), ((), ())), preferred_element_type=F32)


def nn(a, b):
    return lax.dot_general(a, b, (((1,), (0,)), ((), ())), preferred_element_type=F32)


def tn(a, b):
    return lax.dot_general(a, b, (((0,), (0,)), ((), ())), preferred_element_type=F32)


def kernel(
    gain,
    pairs,
    img_ref,
    cur_ref,
    loss_ref,
    dimg_ref,
    dcur_ref,
    I,
    C,
    S,
    W,
    rst,
    cst,
    tot_r,
    tot_c,
    val_r,
    val_c,
    pw,
    pin,
    pown,
    py,
    pyin,
    qo,
    qoin,
    qw,
    qin,
    qown,
    qy,
    qyin,
    ag_i_s,
    ag_i_r,
    ag_c_s,
    ag_c_r,
    co_s,
    co_r,
    st_r_s,
    st_r_r,
    st_c_s,
    st_c_r,
    vl_r_s,
    vl_r_r,
    vl_c_s,
    vl_c_r,
    px_s,
    px_r,
    py_s,
    py_r,
    qo_s,
    qo_r,
    qz_s,
    qz_r,
    qy_s,
    qy_r,
):
    blk, rep = lax.axis_index("blk"), lax.axis_index("rep")
    x = blk % 4
    z = (blk // 4) % 4
    yh = blk // 16
    yl = rep // 2
    c = rep % 2

    def dev(x, yl, z, yh, c):
        return ((yh * 4 + z) * 4 + x, yl * 2 + c)

    def img_dev(dx, dy):
        return dev((x + dx) % 4, (yl + dy) % 2, z, yh, c)

    def cur_dev(dz, dy, dc):
        return dev(x, yl, (z + dz) % 4, (yh + dy) % 2, (c + dc) % 2)

    def copy(src, dst, send, recv, device):
        return pltpu.make_async_remote_copy(
            src_ref=src, dst_ref=dst, send_sem=send, recv_sem=recv, device_id=device, device_id_type=MESH
        )

    img_peers = [(dx, dy) for dx in range(4) for dy in range(2) if dx or dy]
    cur_peers = [(dz, dy, dc) for dz in range(4) for dy in range(2) for dc in range(2) if dz or dy or dc]
    mi = x * 2 + yl
    mc = c * 8 + z * 2 + yh
    half = c * 8
    other = (1 - c) * 8

    barrier = pltpu.get_barrier_semaphore()
    for d in img_peers:
        pl.semaphore_signal(barrier, inc=1, device_id=img_dev(*d), device_id_type=MESH)
    for d in cur_peers:
        pl.semaphore_signal(barrier, inc=1, device_id=cur_dev(*d), device_id_type=MESH)
    pl.semaphore_wait(barrier, len(img_peers) + len(cur_peers))

    pending = []

    def go(cp):
        cp.start()
        pending.append(cp)
        return cp

    iy = go(copy(img_ref, I.at[mi], ag_i_s.at[0], ag_i_r.at[0], img_dev(0, 1)))
    cy = go(copy(cur_ref, C.at[mc], ag_c_s.at[0], ag_c_r.at[0], cur_dev(0, 1, 0)))
    ix, cz = {}, {}
    for d in (1, 3, 2):
        ix[d] = go(copy(img_ref, I.at[mi], ag_i_s.at[d], ag_i_r.at[d], img_dev(d, 0)))
        cz[d] = go(copy(cur_ref, C.at[mc], ag_c_s.at[d], ag_c_r.at[d], cur_dev(d, 0, 0)))
    cores = []

    def forward(slot, k):
        cores.append(go(copy(C.at[slot], C.at[slot], co_s.at[k], co_r.at[k], cur_dev(0, 0, 1))))

    cores.append(go(copy(cur_ref, C.at[mc], co_s.at[0], co_r.at[0], cur_dev(0, 0, 1))))
    I[mi] = img_ref[...]
    C[mc] = cur_ref[...]
    pos = jnp.sum(img_ref[...].astype(F32) * cur_ref[...].astype(F32), axis=1, keepdims=True) * gain
    pos = jnp.sum(pos, axis=0, keepdims=True)
    iy.wait_recv()
    si = x * 2 + 1 - yl
    sc = half + z * 2 + 1 - yh
    for d in (1, 3, 2):
        ix[d + 4] = go(copy(I.at[si], I.at[si], ag_i_s.at[d + 4], ag_i_r.at[d + 4], img_dev(d, 0)))
    cy.wait_recv()
    for d in (1, 3, 2):
        cz[d + 4] = go(copy(C.at[sc], C.at[sc], ag_c_s.at[d + 4], ag_c_r.at[d + 4], cur_dev(d, 0, 0)))
    forward(sc, 1)
    k = 2
    for y, off in ((yh, 0), (1 - yh, 4)):
        for d in (1, 3, 2):
            cz[d + off].wait_recv()
            forward(half + ((z - d) % 4) * 2 + y, k)
            k += 1
    for d in (1, 3, 2, 5, 7, 6):
        ix[d].wait_recv()
    for cp in cores:
        cp.wait_recv()

    def score_step(p, carry):
        cols = C[pl.ds(2 * p, 2)].reshape(256, 1024)
        s = nt(I[...].reshape(1024, 1024), cols) * gain
        S[p] = s
        high = jnp.max(s, axis=0, keepdims=True)
        lse = high + jnp.log(jnp.sum(jnp.exp(s - high), axis=0, keepdims=True))
        cst[mc, pl.ds(2 * p, 1), :] = lse[:, :128]
        cst[mc, pl.ds(2 * p + 1, 1), :] = lse[:, 128:]
        return carry

    lax.fori_loop(0, 8, score_step, 0)
    c_st = []
    for j, d in enumerate(cur_peers):
        c_st.append(go(copy(cst.at[mc], cst.at[mc], st_c_s.at[j], st_c_r.at[j], cur_dev(*d))))

    def chunks(a):
        rows = pl.ds(pl.multiple_of(a * 128, 128), 128)
        return [S[p, rows, h * 128 : (h + 1) * 128] for p in range(8) for h in range(2)]

    def row_step(a, carry):
        parts = chunks(a)
        m = functools.reduce(jnp.maximum, parts)
        total = functools.reduce(jnp.add, [jnp.exp(v - m) for v in parts])
        mt, lt = m.T, total.T
        high = jnp.max(mt, axis=0, keepdims=True)
        lse = high + jnp.log(jnp.sum(lt * jnp.exp(mt - high), axis=0, keepdims=True))
        rst[mi, pl.ds(a, 1), :] = lse
        return carry

    lax.fori_loop(0, 8, row_step, 0)
    rst[mi, 8:16, :] = jnp.broadcast_to(pos, (8, 128))
    r_st = []
    for j, d in enumerate(img_peers):
        r_st.append(go(copy(rst.at[mi], rst.at[mi], st_r_s.at[j], st_r_r.at[j], img_dev(*d))))
    for cp in c_st:
        cp.wait_recv()
    parts = [cst[k] for k in range(16)]
    high = functools.reduce(jnp.maximum, parts)
    tot_c[...] = high + jnp.log(functools.reduce(jnp.add, [jnp.exp(v - high) for v in parts]))
    for cp in r_st:
        cp.wait_recv()
    parts = [rst[k, 0:8, :] for k in range(8)]
    high = functools.reduce(jnp.maximum, parts)
    tot_r[...] = high + jnp.log(functools.reduce(jnp.add, [jnp.exp(v - high) for v in parts]))

    def grand(v):
        return jnp.sum(jnp.sum(v, axis=1, keepdims=True), axis=0, keepdims=True)

    pos_all = functools.reduce(jnp.add, [rst[k, 8:16, :] for k in range(8)])
    val_c[mc] = grand(tot_r[...]) - 2.0 * pos_all
    val_r[mi] = jnp.broadcast_to(grand(tot_c[...]), (8, 128))
    vals = []
    for j, d in enumerate(cur_peers):
        vals.append(go(copy(val_c.at[mc], val_c.at[mc], vl_c_s.at[j], vl_c_r.at[j], cur_dev(*d))))
    for j, d in enumerate(img_peers):
        vals.append(go(copy(val_r.at[mi], val_r.at[mi], vl_r_s.at[j], vl_r_r.at[j], img_dev(*d))))

    def weight_step(a, carry):
        rows = pl.ds(pl.multiple_of(a * 128, 128), 128)
        rl = jnp.broadcast_to(tot_r[pl.ds(a, 1), :], (128, 128)).T
        for p in range(8):
            for h in range(2):
                lanes = slice(h * 128, (h + 1) * 128)
                s = S[p, rows, lanes]
                cl = tot_c[2 * p + h : 2 * p + h + 1, :]
                W[p, rows, lanes] = ((jnp.exp(s - rl) + jnp.exp(s - cl)) * 0.5).astype(BF16)
        return carry

    lax.fori_loop(0, 8, weight_step, 0)

    def curve_part(pair):
        return tn(W[pair], I[...].reshape(1024, 1024))

    qos = []
    for j, d in enumerate((2, 1, 3, 0)):
        zz = (z + d) % 4
        qo[j] = curve_part((1 - c) * 4 + zz).reshape(2, 128, 1024)
        qos.append(go(copy(qo.at[j], qoin.at[j], qo_s.at[j], qo_r.at[j], cur_dev(0, 0, 1))))

    def image_part(xx):
        rows = pl.ds(pl.multiple_of(xx * 256, 256), 256)
        w = jnp.concatenate([W[p, rows, :] for p in range(8)], axis=1)
        return nn(w, C[...].reshape(2048, 1024))

    pxs = []
    for j, d in enumerate(HOPS):
        pw[j] = image_part((x + d) % 4).astype(BF16).reshape(2, 128, 1024)
        pxs.append(go(copy(pw.at[j], pin.at[j], px_s.at[j], px_r.at[j], img_dev(d, 0))))
    pown[...] = image_part(x).reshape(2, 128, 1024)
    qzs = []
    for j, d in enumerate(HOPS):
        part = curve_part(c * 4 + (z + d) % 4).reshape(2, 128, 1024)
        qos[j].wait_recv()
        qw[j] = (part + qoin[j]).astype(BF16)
        qzs.append(go(copy(qw.at[j], qin.at[j], qz_s.at[j], qz_r.at[j], cur_dev(d, 0, 0))))
    part = curve_part(c * 4 + z).reshape(2, 128, 1024)
    qos[3].wait_recv()
    qown[...] = part + qoin[3]

    for cp in pxs:
        cp.wait_recv()
    py[...] = (pown[1 - yl] + sum(pin[j, 1 - yl].astype(F32) for j in range(3))).astype(BF16)
    pys = go(copy(py, pyin, py_s, py_r, img_dev(0, 1)))
    for cp in qzs:
        cp.wait_recv()
    qy[...] = (qown[1 - yh] + sum(qin[j, 1 - yh].astype(F32) for j in range(3))).astype(BF16)
    qys = go(copy(qy, qyin, qy_s, qy_r, cur_dev(0, 1, 0)))
    mine = pown[yl] + sum(pin[j, yl].astype(F32) for j in range(3)) - cur_ref[...].astype(F32)
    pys.wait_recv()
    dimg_ref[...] = (mine + pyin[...].astype(F32)) * gain
    mine = qown[yh] + sum(qin[j, yh].astype(F32) for j in range(3)) - img_ref[...].astype(F32)
    for cp in vals:
        cp.wait_recv()
    total = sum(val_c[k] for k in range(16)) + sum(val_r[k] for k in range(8))
    loss_ref[...] = total[0:1, 0:1] / (2.0 * pairs)
    qys.wait_recv()
    dcur_ref[...] = (mine + qyin[...].astype(F32)) * gain
    for cp in pending:
        cp.wait_send()


def solution(mesh):
    def step(image_emb, curve_emb):
        gain = math.sqrt(image_emb.shape[1])
        vmem = pl.BlockSpec(memory_space=pltpu.VMEM)
        dma = pltpu.SemaphoreType.DMA
        loss, dimg, dcur = pl.pallas_call(
            functools.partial(kernel, gain, 16384),
            out_shape=(
                jax.ShapeDtypeStruct((1, 1), F32),
                jax.ShapeDtypeStruct((128, 1024), F32),
                jax.ShapeDtypeStruct((128, 1024), F32),
            ),
            in_specs=[vmem, vmem],
            out_specs=(vmem, vmem, vmem),
            scratch_shapes=[
                pltpu.VMEM((8, 128, 1024), BF16),
                pltpu.VMEM((16, 128, 1024), BF16),
                pltpu.VMEM((8, 1024, 256), F32),
                pltpu.VMEM((8, 1024, 256), BF16),
                pltpu.VMEM((8, 16, 128), F32),
                pltpu.VMEM((16, 16, 128), F32),
                pltpu.VMEM((8, 128), F32),
                pltpu.VMEM((16, 128), F32),
                pltpu.VMEM((8, 8, 128), F32),
                pltpu.VMEM((16, 8, 128), F32),
                pltpu.VMEM((3, 2, 128, 1024), BF16),
                pltpu.VMEM((3, 2, 128, 1024), BF16),
                pltpu.VMEM((2, 128, 1024), F32),
                pltpu.VMEM((128, 1024), BF16),
                pltpu.VMEM((128, 1024), BF16),
                pltpu.VMEM((4, 2, 128, 1024), F32),
                pltpu.VMEM((4, 2, 128, 1024), F32),
                pltpu.VMEM((3, 2, 128, 1024), BF16),
                pltpu.VMEM((3, 2, 128, 1024), BF16),
                pltpu.VMEM((2, 128, 1024), F32),
                pltpu.VMEM((128, 1024), BF16),
                pltpu.VMEM((128, 1024), BF16),
                dma((8,)), dma((8,)), dma((8,)), dma((8,)), dma((8,)), dma((8,)),
                dma((7,)), dma((7,)), dma((15,)), dma((15,)),
                dma((7,)), dma((7,)), dma((15,)), dma((15,)),
                dma((3,)), dma((3,)), dma, dma,
                dma((4,)), dma((4,)), dma((3,)), dma((3,)), dma, dma,
            ],
            compiler_params=pltpu.CompilerParams(
                collective_id=0, has_side_effects=True, vmem_limit_bytes=60 << 20
            ),
        )(image_emb, curve_emb)
        return loss.reshape(()), dimg, dcur

    spec = P(("blk", "rep"), None)
    return jax.shard_map(step, mesh=mesh, in_specs=(spec, spec), out_specs=(P(), spec, spec), check_vma=False)
```

```python
import functools
import math

import jax
import jax.numpy as jnp
from jax import lax
from jax.experimental import pallas as pl
from jax.experimental.pallas import tpu as pltpu
from jax.sharding import PartitionSpec as P

F32, BF16 = jnp.float32, jnp.bfloat16
MESH = pl.DeviceIdType.MESH
PLACES = ((0, 0), (0, 1), (-1, 0), (1, 0), (2, 0), (-1, 1), (1, 1), (2, 1))
SLOT = {p: k for k, p in enumerate(PLACES)}
HALF = (slice(0, 64), slice(64, 128))
COPIES = 128


def nt(a, b):
    return lax.dot_general(a, b, (((1,), (1,)), ((), ())), preferred_element_type=F32)


def nn(a, b):
    return lax.dot_general(a, b, (((1,), (0,)), ((), ())), preferred_element_type=F32)


def tn(a, b):
    return lax.dot_general(a, b, (((0,), (0,)), ((), ())), preferred_element_type=F32)


def kernel(
    gain,
    pairs,
    img_ref,
    cur_ref,
    loss_ref,
    dimg_ref,
    dcur_ref,
    I,
    C,
    S,
    W,
    RM,
    RL,
    CM,
    CL,
    rst,
    cst,
    tot_r,
    tot_c,
    val_r,
    val_c,
    pw,
    pin,
    pf,
    pown,
    py,
    qo,
    qoin,
    qw,
    qin,
    qf,
    qown,
    qy,
    sends,
    recvs,
):
    blk, rep = lax.axis_index("blk"), lax.axis_index("rep")
    x = blk % 4
    z = (blk // 4) % 4
    yh = blk // 16
    yl = rep // 2
    c = rep % 2

    def dev(x, yl, z, yh, c):
        return ((yh * 4 + z) * 4 + x, yl * 2 + c)

    def img_dev(dx, dy):
        return dev((x + dx + 4) % 4, (yl + dy) % 2, z, yh, c)

    def cur_dev(dz, dy, dc):
        return dev(x, (yl + dy) % 2, (z + dz + 4) % 4, (yh + dy) % 2, (c + dc) % 2)

    count = [0]
    pending = []

    def go(src, dst, device):
        k = count[0]
        count[0] += 1
        cp = pltpu.make_async_remote_copy(
            src_ref=src,
            dst_ref=dst,
            send_sem=sends.at[k],
            recv_sem=recvs.at[k],
            device_id=device,
            device_id_type=MESH,
        )
        cp.start()
        pending.append(cp)
        return cp

    img_peers = [(dx, dy) for dx in range(4) for dy in range(2) if dx or dy]
    cur_peers = [(dz, dy, dc) for dz in range(4) for dy in range(2) for dc in range(2) if dz or dy or dc]

    barrier = pltpu.get_barrier_semaphore()
    near = [img_dev(0, 1), img_dev(1, 0), img_dev(-1, 0)]
    near += [cur_dev(0, 1, 0), cur_dev(1, 0, 0), cur_dev(-1, 0, 0), cur_dev(0, 0, 1)]
    for d in near:
        pl.semaphore_signal(barrier, inc=1, device_id=d, device_id_type=MESH)
    pl.semaphore_wait(barrier, len(near))

    ring = ((1, 0), (-1, 1))
    back = ((1, 1), (-1, 0))
    iy, cy, io, co, ip, cp_, ir, cr = ({} for _ in range(8))
    cores = {}

    def core(slot, h):
        cores[slot, h] = go(C.at[slot, 0, HALF[h]], C.at[slot, 1, HALF[h]], cur_dev(0, 0, 1))

    def send_own(d, h):
        s = SLOT[-d, 0]
        io[d, h] = go(img_ref.at[HALF[h]], I.at[s, HALF[h]], img_dev(d, 0))
        co[d, h] = go(cur_ref.at[HALF[h]], C.at[s, 0, HALF[h]], cur_dev(d, 0, 0))

    def pass_on(d, h, y):
        s, t = SLOT[-d, y], SLOT[2, y]
        ir[d, h, y] = go(I.at[s, HALF[h]], I.at[t, HALF[h]], img_dev(d, 0))
        cr[d, h, y] = go(C.at[s, 0, HALF[h]], C.at[t, 0, HALF[h]], cur_dev(d, 0, 0))

    for h in range(2):
        iy[h] = go(img_ref.at[HALF[h]], I.at[1, HALF[h]], img_dev(0, 1))
        cy[h] = go(cur_ref.at[HALF[h]], C.at[1, 0, HALF[h]], cur_dev(0, 1, 0))
        for d, k in ring if h == 0 else back:
            send_own(d, k)
    own_core = go(cur_ref, C.at[0, 1], cur_dev(0, 0, 1))
    I[0] = img_ref[...]
    C[0, 0] = cur_ref[...]
    pos = jnp.sum(img_ref[...].astype(F32) * cur_ref[...].astype(F32), axis=1, keepdims=True) * gain
    pos = jnp.sum(pos, axis=0, keepdims=True)
    for d, h in ring:
        io[d, h].wait_recv()
        co[d, h].wait_recv()
        pass_on(d, h, 0)
        core(SLOT[-d, 0], h)
    for h in range(2):
        iy[h].wait_recv()
        cy[h].wait_recv()
        for d, k in ring if h == 0 else back:
            ip[d, h] = go(I.at[1, HALF[h]], I.at[SLOT[-d, 1], HALF[h]], img_dev(d, 0))
            cp_[d, h] = go(C.at[1, 0, HALF[h]], C.at[SLOT[-d, 1], 0, HALF[h]], cur_dev(d, 0, 0))
        core(1, h)
        if h == 0:
            for d, k in back:
                io[d, k].wait_recv()
                co[d, k].wait_recv()
                core(SLOT[-d, 0], k)

    def scores(rows, cols):
        r0, r1 = rows

        def step(q, carry):
            a = I[r0:r1].reshape((r1 - r0) * 128, 1024)
            s = nt(a, C[q].reshape(256, 1024)) * gain
            S[q, r0:r1] = s.reshape(r1 - r0, 128, 256)
            return carry

        lax.fori_loop(cols[0], cols[1], step, 0)

    def row_stats(rows, cols, fresh):
        def step(a, carry):
            parts = [S[q, a, :, h * 128 : h * 128 + 128] for q in range(*cols) for h in range(2)]
            m = functools.reduce(jnp.maximum, parts)
            if fresh:
                total = functools.reduce(jnp.add, [jnp.exp(v - m) for v in parts])
            else:
                old = RM[a]
                m = jnp.maximum(m, old)
                total = RL[a] * jnp.exp(old - m)
                total = functools.reduce(jnp.add, [jnp.exp(v - m) for v in parts], total)
            RM[a] = m
            RL[a] = total
            return carry

        lax.fori_loop(rows[0], rows[1], step, 0)

    def col_stats(rows, cols, fresh):
        r0, r1 = rows

        def step(q, carry):
            s = S[q, r0:r1].reshape((r1 - r0) * 16, 8, 256)
            m = jnp.max(s, axis=0)
            if not fresh:
                old = CM[q]
                m = jnp.maximum(m, old)
            total = jnp.sum(jnp.exp(s - m[None]), axis=0)
            if not fresh:
                total = total + CL[q] * jnp.exp(old - m)
            CM[q] = m
            CL[q] = total
            return carry

        lax.fori_loop(cols[0], cols[1], step, 0)

    for d, h in ring + back:
        cores[SLOT[-d, 0], h].wait_recv()
    own_core.wait_recv()
    cores[1, 0].wait_recv()
    cores[1, 1].wait_recv()
    scores((0, 4), (0, 4))
    row_stats((0, 4), (0, 4), True)
    col_stats((0, 4), (0, 4), True)
    for d, h in ring:
        ir[d, h, 0].wait_recv()
        cr[d, h, 0].wait_recv()
        core(SLOT[2, 0], h)
    for d, h in ring:
        ip[d, h].wait_recv()
        cp_[d, h].wait_recv()
        pass_on(d, h, 1)
        core(SLOT[-d, 1], h)
    for d, h in back:
        ip[d, h].wait_recv()
        cp_[d, h].wait_recv()
        core(SLOT[-d, 1], h)
    for d, h in ring + back:
        cores[SLOT[-d, 1], h].wait_recv()
    for h in range(2):
        cores[SLOT[2, 0], h].wait_recv()
    scores((4, 7), (0, 4))
    scores((0, 7), (4, 7))
    for d, h in ring:
        ir[d, h, 1].wait_recv()
        cr[d, h, 1].wait_recv()
        core(SLOT[2, 1], h)
    row_stats((0, 4), (4, 7), False)
    row_stats((4, 7), (0, 7), True)
    col_stats((4, 7), (0, 4), False)
    col_stats((0, 7), (4, 7), True)
    for h in range(2):
        cores[SLOT[2, 1], h].wait_recv()
    scores((7, 8), (0, 7))
    scores((0, 8), (7, 8))
    row_stats((0, 7), (7, 8), False)
    row_stats((7, 8), (0, 8), True)
    col_stats((7, 8), (0, 7), False)
    col_stats((0, 8), (7, 8), True)

    def img_place(dx, dy):
        return ((x + dx + 4) % 4) * 2 + (yl + dy) % 2

    def cur_place(dz, dy, dc):
        return ((c + dc) % 2) * 8 + ((z + dz + 4) % 4) * 2 + (yh + dy) % 2

    mi = img_place(0, 0)
    mc = cur_place(0, 0, 0)
    for q, (dz, dy) in enumerate(PLACES):
        m = CM[q]
        high = jnp.max(m, axis=0, keepdims=True)
        lse = high + jnp.log(jnp.sum(CL[q] * jnp.exp(m - high), axis=0, keepdims=True))
        cst[mc, pl.ds(cur_place(dz, dy, 0), 1), :] = lse[:, :128]
        cst[mc, pl.ds(cur_place(dz, dy, 1), 1), :] = lse[:, 128:]
    c_st = [go(cst.at[mc], cst.at[mc], cur_dev(*d)) for d in cur_peers]
    for a, (dx, dy) in enumerate(PLACES):
        m = RM[a].T
        high = jnp.max(m, axis=0, keepdims=True)
        lse = high + jnp.log(jnp.sum(RL[a].T * jnp.exp(m - high), axis=0, keepdims=True))
        rst[mi, pl.ds(img_place(dx, dy), 1), :] = lse
    rst[mi, 8:16, :] = jnp.broadcast_to(pos, (8, 128))
    r_st = [go(rst.at[mi], rst.at[mi], img_dev(*d)) for d in img_peers]
    for cp in r_st:
        cp.wait_recv()
    parts = [rst[k, 0:8, :] for k in range(8)]
    high = functools.reduce(jnp.maximum, parts)
    tot_r[...] = high + jnp.log(functools.reduce(jnp.add, [jnp.exp(v - high) for v in parts]))
    for a, (dx, dy) in enumerate(PLACES):
        RM[a] = jnp.broadcast_to(tot_r[pl.ds(img_place(dx, dy), 1), :], (128, 128)).T
    for cp in c_st:
        cp.wait_recv()
    parts = [cst[k] for k in range(16)]
    high = functools.reduce(jnp.maximum, parts)
    tot_c[...] = high + jnp.log(functools.reduce(jnp.add, [jnp.exp(v - high) for v in parts]))

    for q, (dz, dy) in enumerate(PLACES):
        for h in range(2):
            CM[q, :, h * 128 : h * 128 + 128] = jnp.broadcast_to(tot_c[pl.ds(cur_place(dz, dy, h), 1), :], (8, 128))

    def weight_step(a, carry):
        rl = RM[a]
        for q in range(8):
            for h in range(2):
                lanes = slice(h * 128, h * 128 + 128)
                s = S[q, a, :, lanes]
                cl = CM[q, 0:1, lanes]
                W[q, a, :, lanes] = ((jnp.exp(s - rl) + jnp.exp(s - cl)) * 0.5).astype(BF16)
        return carry

    lax.fori_loop(0, 8, weight_step, 0)

    swaps = {}
    curve_f32 = {}

    def curve_part(q):
        part = tn(W[q].reshape(1024, 256), I[...].reshape(1024, 1024))
        qo[q, 1] = part[128:256]
        swaps[q] = go(qo.at[q, 1], qoin.at[q], cur_dev(0, 0, 1))
        qo[q, 0] = part[0:128]

    def joined(q):
        swaps[q].wait_recv()
        return qo[q, 0] + qoin[q]

    def image_part(a1, a2):
        w = jnp.concatenate(
            [jnp.concatenate([W[q, a] for q in range(8)], axis=1) for a in (a1, a2)], axis=0
        )
        return nn(w, C[...].reshape(2048, 1024))

    hops = {}

    def far(kind, y, part):
        w, into, to = (pw, pin, lambda d: img_dev(d, 0)) if kind == "i" else (qw, qin, lambda d: cur_dev(d, 0, 0))
        w[y, 0] = part.astype(BF16)
        for d, h in ring:
            hops[kind, y, "far", d] = go(w.at[y, 0, HALF[h]], into.at[y, 0, HALF[h]], to(d))

    def near_first(kind, y, d, part):
        w, into, keep, to = (
            (pw, pin, pf, lambda d: img_dev(d, 0)) if kind == "i" else (qw, qin, qf, lambda d: cur_dev(d, 0, 0))
        )
        k = 1 if d == 1 else 2
        through = 0 if d == 1 else 1
        rest = 1 - through
        w[y, k, HALF[rest]] = part[HALF[rest]].astype(BF16)
        hops[kind, y, "rest", d] = go(w.at[y, k, HALF[rest]], into.at[y, k, HALF[rest]], to(d))
        keep[y, k - 1] = part[HALF[through]]

    def near_second(kind, y):
        w, into, keep, to = (
            (pw, pin, pf, lambda d: img_dev(d, 0)) if kind == "i" else (qw, qin, qf, lambda d: cur_dev(d, 0, 0))
        )
        for d, h in ring:
            k = 1 if d == 1 else 2
            hops[kind, y, "far", d].wait_recv()
            w[y, k, HALF[h]] = (keep[y, k - 1] + into[y, 0, HALF[h]].astype(F32)).astype(BF16)
            hops[kind, y, "through", d] = go(w.at[y, k, HALF[h]], into.at[y, k, HALF[h]], to(d))

    def collected(kind, y):
        into, own = (pin, pown) if kind == "i" else (qin, qown)
        for d in (1, -1):
            hops[kind, y, "rest", d].wait_recv()
            hops[kind, y, "through", d].wait_recv()
        return own[y] + into[y, 1].astype(F32) + into[y, 2].astype(F32)

    curve_part(SLOT[2, 1])
    curve_part(SLOT[2, 0])
    part = image_part(SLOT[2, 1], SLOT[2, 0])
    far("i", 1, part[0:128])
    far("i", 0, part[128:256])
    curve_part(SLOT[1, 1])
    curve_part(SLOT[-1, 1])
    far("c", 1, joined(SLOT[2, 1]))
    far("c", 0, joined(SLOT[2, 0]))
    part = image_part(SLOT[1, 1], SLOT[-1, 1])
    near_first("i", 1, 1, part[0:128])
    near_first("i", 1, -1, part[128:256])
    near_first("c", 1, 1, joined(SLOT[1, 1]))
    near_first("c", 1, -1, joined(SLOT[-1, 1]))
    curve_part(SLOT[1, 0])
    curve_part(SLOT[-1, 0])
    near_second("i", 1)
    part = image_part(SLOT[1, 0], SLOT[-1, 0])
    near_first("i", 0, 1, part[0:128])
    near_first("i", 0, -1, part[128:256])
    near_second("c", 1)
    near_first("c", 0, 1, joined(SLOT[1, 0]))
    near_first("c", 0, -1, joined(SLOT[-1, 0]))
    curve_part(SLOT[0, 1])
    curve_part(SLOT[0, 0])
    near_second("i", 0)
    near_second("c", 0)
    part = image_part(SLOT[0, 1], SLOT[0, 0])
    pown[1] = part[0:128]
    pown[0] = part[128:256]
    qown[1] = joined(SLOT[0, 1])
    qown[0] = joined(SLOT[0, 0])

    py[0] = collected("i", 1).astype(BF16)
    pys = go(py.at[0], py.at[1], img_dev(0, 1))
    qy[0] = collected("c", 1).astype(BF16)
    qys = go(qy.at[0], qy.at[1], cur_dev(0, 1, 0))

    def grand(v):
        return jnp.sum(jnp.sum(v, axis=1, keepdims=True), axis=0, keepdims=True)

    pos_all = functools.reduce(jnp.add, [rst[k, 8:16, :] for k in range(8)])
    val_c[mc] = grand(tot_r[...]) - 2.0 * pos_all
    val_r[mi] = jnp.broadcast_to(grand(tot_c[...]), (8, 128))
    vals = [go(val_c.at[mc], val_c.at[mc], cur_dev(*d)) for d in cur_peers]
    vals += [go(val_r.at[mi], val_r.at[mi], img_dev(*d)) for d in img_peers]

    pown[0] = collected("i", 0) - cur_ref[...].astype(F32)
    qown[0] = collected("c", 0) - img_ref[...].astype(F32)
    for cp in vals:
        cp.wait_recv()
    total = sum(val_c[k] for k in range(16)) + sum(val_r[k] for k in range(8))
    loss_ref[...] = total[0:1, 0:1] / (2.0 * pairs)
    pys.wait_recv()
    dimg_ref[...] = (pown[0] + py[1].astype(F32)) * gain
    qys.wait_recv()
    dcur_ref[...] = (qown[0] + qy[1].astype(F32)) * gain
    for cp in pending:
        cp.wait_send()


def solution(mesh):
    def step(image_emb, curve_emb):
        gain = math.sqrt(image_emb.shape[1])
        vmem = pl.BlockSpec(memory_space=pltpu.VMEM)
        loss, dimg, dcur = pl.pallas_call(
            functools.partial(kernel, gain, 16384),
            out_shape=(
                jax.ShapeDtypeStruct((1, 1), F32),
                jax.ShapeDtypeStruct((128, 1024), F32),
                jax.ShapeDtypeStruct((128, 1024), F32),
            ),
            in_specs=[vmem, vmem],
            out_specs=(vmem, vmem, vmem),
            scratch_shapes=[
                pltpu.VMEM((8, 128, 1024), BF16),
                pltpu.VMEM((8, 2, 128, 1024), BF16),
                pltpu.VMEM((8, 8, 128, 256), F32),
                pltpu.VMEM((8, 8, 128, 256), BF16),
                pltpu.VMEM((8, 128, 128), F32),
                pltpu.VMEM((8, 128, 128), F32),
                pltpu.VMEM((8, 8, 256), F32),
                pltpu.VMEM((8, 8, 256), F32),
                pltpu.VMEM((8, 16, 128), F32),
                pltpu.VMEM((16, 16, 128), F32),
                pltpu.VMEM((8, 128), F32),
                pltpu.VMEM((16, 128), F32),
                pltpu.VMEM((8, 8, 128), F32),
                pltpu.VMEM((16, 8, 128), F32),
                pltpu.VMEM((2, 3, 128, 1024), BF16),
                pltpu.VMEM((2, 3, 128, 1024), BF16),
                pltpu.VMEM((2, 2, 64, 1024), F32),
                pltpu.VMEM((2, 128, 1024), F32),
                pltpu.VMEM((2, 128, 1024), BF16),
                pltpu.VMEM((8, 2, 128, 1024), F32),
                pltpu.VMEM((8, 128, 1024), F32),
                pltpu.VMEM((2, 3, 128, 1024), BF16),
                pltpu.VMEM((2, 3, 128, 1024), BF16),
                pltpu.VMEM((2, 2, 64, 1024), F32),
                pltpu.VMEM((2, 128, 1024), F32),
                pltpu.VMEM((2, 128, 1024), BF16),
                pltpu.SemaphoreType.DMA((COPIES,)),
                pltpu.SemaphoreType.DMA((COPIES,)),
            ],
            compiler_params=pltpu.CompilerParams(
                collective_id=0, has_side_effects=True, vmem_limit_bytes=60 << 20
            ),
        )(image_emb, curve_emb)
        return loss.reshape(()), dimg, dcur

    spec = P(("blk", "rep"), None)
    return jax.shard_map(step, mesh=mesh, in_specs=(spec, spec), out_specs=(P(), spec, spec), check_vma=False)
```

```python
import functools
import math

import jax
import jax.numpy as jnp
from jax import lax
from jax.experimental import pallas as pl
from jax.experimental.pallas import tpu as pltpu
from jax.sharding import PartitionSpec as P

F32, BF16 = jnp.float32, jnp.bfloat16
MESH = pl.DeviceIdType.MESH
PLACES = ((0, 0), (0, 1), (-1, 0), (1, 0), (2, 0), (-1, 1), (1, 1), (2, 1))
SLOT = {p: k for k, p in enumerate(PLACES)}
HALF = (slice(0, 64), slice(64, 128))


def nt(a, b):
    return lax.dot_general(a, b, (((1,), (1,)), ((), ())), preferred_element_type=F32)


def nn(a, b):
    return lax.dot_general(a, b, (((1,), (0,)), ((), ())), preferred_element_type=F32)


def tn(a, b):
    return lax.dot_general(a, b, (((0,), (0,)), ((), ())), preferred_element_type=F32)


def kernel(
    gain,
    pairs,
    img_ref,
    cur_ref,
    loss_ref,
    dimg_ref,
    dcur_ref,
    I,
    C,
    S,
    W,
    RM,
    RL,
    CM,
    CL,
    rst,
    cst,
    tot_r,
    tot_c,
    val_r,
    val_c,
    pw,
    pin,
    pf,
    pa,
    pown,
    py,
    qo,
    qoin,
    qw,
    qin,
    qf,
    qa,
    qown,
    qy,
    sends,
    recvs,
):
    blk, rep = lax.axis_index("blk"), lax.axis_index("rep")
    x = blk % 4
    z = (blk // 4) % 4
    yh = blk // 16
    yl = rep // 2
    c = rep % 2

    def dev(x, yl, z, yh, c):
        return ((yh * 4 + z) * 4 + x, yl * 2 + c)

    def img_dev(dx, dy):
        return dev((x + dx + 4) % 4, (yl + dy) % 2, z, yh, c)

    def cur_dev(dz, dy, dc):
        return dev(x, (yl + dy) % 2, (z + dz + 4) % 4, (yh + dy) % 2, (c + dc) % 2)

    def go(src, dst, device, send, recv):
        pltpu.make_async_remote_copy(
            src_ref=src,
            dst_ref=dst,
            send_sem=sends.at[send],
            recv_sem=recvs.at[recv],
            device_id=device,
            device_id_type=MESH,
        ).start()

    def got(recv, size):
        pltpu.make_async_copy(size, size, recvs.at[recv]).wait()

    def left(send, size):
        pltpu.make_async_copy(size, size, sends.at[send]).wait()

    img_peers = [(dx, dy) for dx in range(4) for dy in range(2) if dx or dy]
    cur_peers = [(dz, dy, dc) for dz in range(4) for dy in range(2) for dc in range(2) if dz or dy or dc]

    barrier = pltpu.get_barrier_semaphore()
    near = [img_dev(0, 1), img_dev(1, 0), img_dev(-1, 0)]
    near += [cur_dev(0, 1, 0), cur_dev(1, 0, 0), cur_dev(-1, 0, 0), cur_dev(0, 0, 1)]
    for d in near:
        pl.semaphore_signal(barrier, inc=1, device_id=d, device_id_type=MESH)
    pl.semaphore_wait(barrier, len(near))

    ring = ((1, 0), (-1, 1))
    back = ((1, 1), (-1, 0))
    G_Y, G_OWN, G_FAR, G_P, G_LAST, G_CORE = 0, 2, 6, 8, 10, 12

    def core(slot, h, group):
        go(C.at[slot, 0, HALF[h]], C.at[slot, 1, HALF[h]], cur_dev(0, 0, 1), 1, G_CORE + group)

    def both(i_src, c_src, slot, h, d, y, recv):
        go(i_src, I.at[slot, HALF[h]], img_dev(d, y), 0, recv)
        go(c_src, C.at[slot, 0, HALF[h]], cur_dev(d, y, 0), 0, recv)

    def onward(slot, to, h, d, y, recv):
        both(I.at[slot, HALF[h]], C.at[slot, 0, HALF[h]], to, h, d, y, recv)

    def own_sem(d, h):
        return G_OWN + (d + 1) + h

    for h in range(2):
        both(img_ref.at[HALF[h]], cur_ref.at[HALF[h]], 1, h, 0, 1, G_Y + h)
        for d, k in ring if h == 0 else back:
            both(img_ref.at[HALF[k]], cur_ref.at[HALF[k]], SLOT[-d, 0], k, d, 0, own_sem(d, k))
    go(cur_ref, C.at[0, 1], cur_dev(0, 0, 1), 1, G_CORE)
    I[0] = img_ref[...]
    C[0, 0] = cur_ref[...]
    pos = jnp.sum(img_ref[...].astype(F32) * cur_ref[...].astype(F32), axis=1, keepdims=True) * gain
    pos = jnp.sum(pos, axis=0, keepdims=True)
    for d, h in ring:
        got(own_sem(d, h), I.at[0])
        onward(SLOT[-d, 0], SLOT[2, 0], h, d, 0, G_FAR + h)
        core(SLOT[-d, 0], h, 0)
    for h in range(2):
        got(G_Y + h, I.at[0])
        for d, k in ring if h == 0 else back:
            onward(1, SLOT[-d, 1], h, d, 0, G_P + h)
        core(1, h, 0)
        if h == 0:
            for d, k in back:
                got(own_sem(d, k), I.at[0])
                core(SLOT[-d, 0], k, 0)

    def scores(rows, cols):
        r0, r1 = rows

        def step(q, carry):
            a = I[r0:r1].reshape((r1 - r0) * 128, 1024)
            s = nt(a, C[q].reshape(256, 1024)) * gain
            S[q, r0:r1] = s.reshape(r1 - r0, 128, 256)
            return carry

        lax.fori_loop(cols[0], cols[1], step, 0)

    def row_stats(rows, cols, fresh):
        def step(a, carry):
            parts = [S[q, a, :, h * 128 : h * 128 + 128] for q in range(*cols) for h in range(2)]
            m = functools.reduce(jnp.maximum, parts)
            if fresh:
                total = functools.reduce(jnp.add, [jnp.exp(v - m) for v in parts])
            else:
                old = RM[a]
                m = jnp.maximum(m, old)
                total = RL[a] * jnp.exp(old - m)
                total = functools.reduce(jnp.add, [jnp.exp(v - m) for v in parts], total)
            RM[a] = m
            RL[a] = total
            return carry

        lax.fori_loop(rows[0], rows[1], step, 0)

    def col_stats(rows, cols, fresh):
        r0, r1 = rows

        def step(q, carry):
            s = S[q, r0:r1].reshape((r1 - r0) * 16, 8, 256)
            m = jnp.max(s, axis=0)
            if not fresh:
                old = CM[q]
                m = jnp.maximum(m, old)
            total = jnp.sum(jnp.exp(s - m[None]), axis=0)
            if not fresh:
                total = total + CL[q] * jnp.exp(old - m)
            CM[q] = m
            CL[q] = total
            return carry

        lax.fori_loop(cols[0], cols[1], step, 0)

    got(G_CORE, S.at[0])
    scores((0, 4), (0, 4))
    for h in range(2):
        got(G_FAR + h, I.at[0])
        onward(SLOT[2, 0], SLOT[2, 1], h, 0, 1, G_LAST + h)
        core(SLOT[2, 0], h, 1)
    for h in range(2):
        got(G_P + h, I.at[0:2])
        core(SLOT[1, 1], h, 1)
        core(SLOT[-1, 1], h, 1)
    row_stats((0, 4), (0, 4), True)
    col_stats((0, 4), (0, 4), True)
    got(G_CORE + 1, S.at[0, 0:6])
    scores((4, 7), (0, 4))
    scores((0, 7), (4, 7))
    for h in range(2):
        got(G_LAST + h, I.at[0])
        core(SLOT[2, 1], h, 2)
    row_stats((0, 4), (4, 7), False)
    row_stats((4, 7), (0, 7), True)
    col_stats((4, 7), (0, 4), False)
    col_stats((0, 7), (4, 7), True)
    got(G_CORE + 2, I.at[0])
    scores((7, 8), (0, 7))
    scores((0, 8), (7, 8))
    row_stats((0, 7), (7, 8), False)
    row_stats((7, 8), (0, 8), True)
    col_stats((7, 8), (0, 7), False)
    col_stats((0, 8), (7, 8), True)

    def img_place(dx, dy):
        return ((x + dx + 4) % 4) * 2 + (yl + dy) % 2

    def cur_place(dz, dy, dc):
        return ((c + dc) % 2) * 8 + ((z + dz + 4) % 4) * 2 + (yh + dy) % 2

    mi = img_place(0, 0)
    mc = cur_place(0, 0, 0)
    for q, (dz, dy) in enumerate(PLACES):
        m = CM[q]
        high = jnp.max(m, axis=0, keepdims=True)
        lse = high + jnp.log(jnp.sum(CL[q] * jnp.exp(m - high), axis=0, keepdims=True))
        cst[mc, pl.ds(cur_place(dz, dy, 0), 1), :] = lse[:, :128]
        cst[mc, pl.ds(cur_place(dz, dy, 1), 1), :] = lse[:, 128:]
    for d in cur_peers:
        go(cst.at[mc], cst.at[mc], cur_dev(*d), 2, 15)
    for a, (dx, dy) in enumerate(PLACES):
        m = RM[a].T
        high = jnp.max(m, axis=0, keepdims=True)
        lse = high + jnp.log(jnp.sum(RL[a].T * jnp.exp(m - high), axis=0, keepdims=True))
        rst[mi, pl.ds(img_place(dx, dy), 1), :] = lse
    rst[mi, 8:16, :] = jnp.broadcast_to(pos, (8, 128))
    for d in img_peers:
        go(rst.at[mi], rst.at[mi], img_dev(*d), 3, 16)
    got(16, rst.at[0:7])
    parts = [rst[k, 0:8, :] for k in range(8)]
    high = functools.reduce(jnp.maximum, parts)
    tot_r[...] = high + jnp.log(functools.reduce(jnp.add, [jnp.exp(v - high) for v in parts]))
    for a, (dx, dy) in enumerate(PLACES):
        RM[a] = jnp.broadcast_to(tot_r[pl.ds(img_place(dx, dy), 1), :], (128, 128)).T
    got(15, cst.at[0:15])
    parts = [cst[k] for k in range(16)]
    high = functools.reduce(jnp.maximum, parts)
    tot_c[...] = high + jnp.log(functools.reduce(jnp.add, [jnp.exp(v - high) for v in parts]))

    for q, (dz, dy) in enumerate(PLACES):
        for h in range(2):
            CM[q, :, h * 128 : h * 128 + 128] = jnp.broadcast_to(tot_c[pl.ds(cur_place(dz, dy, h), 1), :], (8, 128))

    def weight_step(a, carry):
        rl = RM[a]
        for q in range(8):
            for h in range(2):
                lanes = slice(h * 128, h * 128 + 128)
                s = S[q, a, :, lanes]
                cl = CM[q, 0:1, lanes]
                W[q, a, :, lanes] = ((jnp.exp(s - rl) + jnp.exp(s - cl)) * 0.5).astype(BF16)
        return carry

    lax.fori_loop(0, 8, weight_step, 0)

    R_SWAP = 17

    def curve_part(q):
        part = tn(W[q].reshape(1024, 256), I[...].reshape(1024, 1024))
        qo[q, 1] = part[128:256]
        go(qo.at[q, 1], qoin.at[q], cur_dev(0, 0, 1), 4, R_SWAP + q)
        qo[q, 0] = part[0:128]

    def joined(q):
        got(R_SWAP + q, qoin.at[q])
        return qo[q, 0] + qoin[q]

    def image_part(a1, a2):
        w = jnp.concatenate(
            [jnp.concatenate([W[q, a] for q in range(8)], axis=1) for a in (a1, a2)], axis=0
        )
        return nn(w, C[...].reshape(2048, 1024))

    class Side:
        def __init__(self, w, into, keep, far, own, last, base, send, to):
            self.w, self.into, self.keep, self.far, self.own, self.last = w, into, keep, far, own, last
            self.base, self.send, self.to = base, send, to

        def go(self, y, k, h, d, dy, recv):
            go(self.w.at[y, k, h], self.into.at[y, k, h], self.to(d, dy), self.send, self.base + recv)

        def across(self, part):
            self.w[1, 0] = part.astype(BF16)
            for h in range(2):
                self.go(1, 0, HALF[h], 0, 1, h)

        def straight(self, d, part):
            k = 1 if d == 1 else 2
            self.w[1, k] = part.astype(BF16)
            self.go(1, k, slice(0, 128), d, 0, 2)

        def two_steps(self):
            for d, h in ring:
                got(self.base + h, py.at[0, HALF[0]])
                self.w[0, 0, HALF[h]] = (self.far[HALF[h]] + self.into[1, 0, HALF[h]].astype(F32)).astype(BF16)
                self.go(0, 0, HALF[h], d, 0, 3 + h)

        def first_half(self, d, part):
            k, through = (1, 0) if d == 1 else (2, 1)
            rest = HALF[1 - through]
            self.w[0, k, rest] = part[rest].astype(BF16)
            self.go(0, k, rest, d, 0, 5)
            self.keep[k - 1] = part[HALF[through]]

        def second_half(self):
            for d, h in ring:
                k = 1 if d == 1 else 2
                got(self.base + 3 + h, py.at[0, HALF[0]])
                self.w[0, k, HALF[h]] = (self.keep[k - 1] + self.into[0, 0, HALF[h]].astype(F32)).astype(BF16)
                self.go(0, k, HALF[h], d, 0, 5)

        def finish_partner(self):
            got(self.base + 2, I.at[0:2])
            self.last[0] = (self.own[1] + self.into[1, 1].astype(F32) + self.into[1, 2].astype(F32)).astype(BF16)
            go(self.last.at[0], self.last.at[1], self.to(0, 1), self.send, self.base + 6)

        def finish_own(self, other):
            got(self.base + 5, I.at[0:2])
            self.own[0] = self.own[0] + self.into[0, 1].astype(F32) + self.into[0, 2].astype(F32) - other

        def result(self):
            got(self.base + 6, I.at[0])
            return (self.own[0] + self.last[1].astype(F32)) * gain

    img = Side(pw, pin, pf, pa, pown, py, 25, 5, img_dev)
    cur = Side(qw, qin, qf, qa, qown, qy, 32, 5, lambda d, dy: cur_dev(d, dy, 0))

    curve_part(SLOT[2, 1])
    curve_part(SLOT[2, 0])
    part = image_part(SLOT[2, 1], SLOT[2, 0])
    img.across(part[0:128])
    pa[...] = part[128:256]
    cur.across(joined(SLOT[2, 1]))
    curve_part(SLOT[1, 1])
    curve_part(SLOT[-1, 1])
    part = image_part(SLOT[1, 1], SLOT[-1, 1])
    img.straight(1, part[0:128])
    img.straight(-1, part[128:256])
    cur.straight(1, joined(SLOT[1, 1]))
    cur.straight(-1, joined(SLOT[-1, 1]))
    qa[...] = joined(SLOT[2, 0])
    curve_part(SLOT[1, 0])
    curve_part(SLOT[-1, 0])
    img.two_steps()
    part = image_part(SLOT[1, 0], SLOT[-1, 0])
    cur.two_steps()
    img.first_half(1, part[0:128])
    img.first_half(-1, part[128:256])
    cur.first_half(1, joined(SLOT[1, 0]))
    cur.first_half(-1, joined(SLOT[-1, 0]))
    curve_part(SLOT[0, 1])
    curve_part(SLOT[0, 0])
    part = image_part(SLOT[0, 1], SLOT[0, 0])
    pown[1] = part[0:128]
    pown[0] = part[128:256]
    qown[1] = joined(SLOT[0, 1])
    qown[0] = joined(SLOT[0, 0])
    img.finish_partner()
    cur.finish_partner()
    img.second_half()
    cur.second_half()

    def grand(v):
        return jnp.sum(jnp.sum(v, axis=1, keepdims=True), axis=0, keepdims=True)

    pos_all = functools.reduce(jnp.add, [rst[k, 8:16, :] for k in range(8)])
    val_c[mc] = grand(tot_r[...]) - 2.0 * pos_all
    val_r[mi] = jnp.broadcast_to(grand(tot_c[...]), (8, 128))
    for d in cur_peers:
        go(val_c.at[mc], val_c.at[mc], cur_dev(*d), 6, 39)
    for d in img_peers:
        go(val_r.at[mi], val_r.at[mi], img_dev(*d), 7, 40)

    img.finish_own(cur_ref[...].astype(F32))
    cur.finish_own(img_ref[...].astype(F32))
    got(39, val_c.at[0:15])
    got(40, val_r.at[0:7])
    total = sum(val_c[k] for k in range(16)) + sum(val_r[k] for k in range(8))
    loss_ref[...] = total[0:1, 0:1] / (2.0 * pairs)
    dimg_ref[...] = img.result()
    dcur_ref[...] = cur.result()
    left(0, S.at[0:4, 0:7])
    left(1, S.at[0:2])
    left(2, cst.at[0:15])
    left(3, rst.at[0:7])
    left(4, S.at[0:4])
    left(5, S.at[0:4, 0:7])
    left(6, val_c.at[0:15])
    left(7, val_r.at[0:7])


def solution(mesh):
    def step(image_emb, curve_emb):
        gain = math.sqrt(image_emb.shape[1])
        vmem = pl.BlockSpec(memory_space=pltpu.VMEM)
        loss, dimg, dcur = pl.pallas_call(
            functools.partial(kernel, gain, 16384),
            out_shape=(
                jax.ShapeDtypeStruct((1, 1), F32),
                jax.ShapeDtypeStruct((128, 1024), F32),
                jax.ShapeDtypeStruct((128, 1024), F32),
            ),
            in_specs=[vmem, vmem],
            out_specs=(vmem, vmem, vmem),
            scratch_shapes=[
                pltpu.VMEM((8, 128, 1024), BF16),
                pltpu.VMEM((8, 2, 128, 1024), BF16),
                pltpu.VMEM((8, 8, 128, 256), F32),
                pltpu.VMEM((8, 8, 128, 256), BF16),
                pltpu.VMEM((8, 128, 128), F32),
                pltpu.VMEM((8, 128, 128), F32),
                pltpu.VMEM((8, 8, 256), F32),
                pltpu.VMEM((8, 8, 256), F32),
                pltpu.VMEM((8, 16, 128), F32),
                pltpu.VMEM((16, 16, 128), F32),
                pltpu.VMEM((8, 128), F32),
                pltpu.VMEM((16, 128), F32),
                pltpu.VMEM((8, 8, 128), F32),
                pltpu.VMEM((16, 8, 128), F32),
                pltpu.VMEM((2, 3, 128, 1024), BF16),
                pltpu.VMEM((2, 3, 128, 1024), BF16),
                pltpu.VMEM((2, 64, 1024), F32),
                pltpu.VMEM((128, 1024), F32),
                pltpu.VMEM((2, 128, 1024), F32),
                pltpu.VMEM((2, 128, 1024), BF16),
                pltpu.VMEM((8, 2, 128, 1024), F32),
                pltpu.VMEM((8, 128, 1024), F32),
                pltpu.VMEM((2, 3, 128, 1024), BF16),
                pltpu.VMEM((2, 3, 128, 1024), BF16),
                pltpu.VMEM((2, 64, 1024), F32),
                pltpu.VMEM((128, 1024), F32),
                pltpu.VMEM((2, 128, 1024), F32),
                pltpu.VMEM((2, 128, 1024), BF16),
                pltpu.SemaphoreType.DMA((8,)),
                pltpu.SemaphoreType.DMA((41,)),
            ],
            compiler_params=pltpu.CompilerParams(
                collective_id=0, has_side_effects=True, vmem_limit_bytes=48 << 20
            ),
        )(image_emb, curve_emb)
        return loss.reshape(()), dimg, dcur

    spec = P(("blk", "rep"), None)
    return jax.shard_map(step, mesh=mesh, in_specs=(spec, spec), out_specs=(P(), spec, spec), check_vma=False)
```

```python
import functools
import math

import jax
import jax.numpy as jnp
from jax import lax
from jax.experimental import pallas as pl
from jax.experimental.pallas import tpu as pltpu
from jax.sharding import PartitionSpec as P

F32, BF16 = jnp.float32, jnp.bfloat16
MESH = pl.DeviceIdType.MESH
PLACES = ((0, 0), (0, 1), (-1, 0), (1, 0), (2, 0), (-1, 1), (1, 1), (2, 1))
SLOT = {p: k for k, p in enumerate(PLACES)}
HALF = (slice(0, 64), slice(64, 128))


def nt(a, b):
    return lax.dot_general(a, b, (((1,), (1,)), ((), ())), preferred_element_type=F32)


def nn(a, b):
    return lax.dot_general(a, b, (((1,), (0,)), ((), ())), preferred_element_type=F32)


def tn(a, b):
    return lax.dot_general(a, b, (((0,), (0,)), ((), ())), preferred_element_type=F32)


def kernel(
    gain,
    pairs,
    img_ref,
    cur_ref,
    loss_ref,
    dimg_ref,
    dcur_ref,
    I,
    C,
    S,
    W,
    RM,
    RL,
    CM,
    CL,
    rst,
    cst,
    tot_r,
    tot_c,
    val_r,
    val_c,
    pw,
    pin,
    pf,
    pa,
    pown,
    py,
    qo,
    qoin,
    qw,
    qin,
    qf,
    qa,
    qown,
    qy,
    sends,
    recvs,
):
    blk, rep = lax.axis_index("blk"), lax.axis_index("rep")
    x = blk % 4
    z = (blk // 4) % 4
    yh = blk // 16
    yl = rep // 2
    c = rep % 2

    def dev(x, yl, z, yh, c):
        return ((yh * 4 + z) * 4 + x, yl * 2 + c)

    def img_dev(dx, dy):
        return dev((x + dx + 4) % 4, (yl + dy) % 2, z, yh, c)

    def cur_dev(dz, dy, dc):
        return dev(x, (yl + dy) % 2, (z + dz + 4) % 4, (yh + dy) % 2, (c + dc) % 2)

    def go(src, dst, device, send, recv):
        pltpu.make_async_remote_copy(
            src_ref=src,
            dst_ref=dst,
            send_sem=sends.at[send],
            recv_sem=recvs.at[recv],
            device_id=device,
            device_id_type=MESH,
        ).start()

    def got(recv, size):
        pltpu.make_async_copy(size, size, recvs.at[recv]).wait()

    def left(send, size):
        pltpu.make_async_copy(size, size, sends.at[send]).wait()

    img_peers = [(dx, dy) for dx in range(4) for dy in range(2) if dx or dy]
    cur_peers = [(dz, dy, dc) for dz in range(4) for dy in range(2) for dc in range(2) if dz or dy or dc]

    barrier = pltpu.get_barrier_semaphore()
    near = [img_dev(0, 1), img_dev(1, 0), img_dev(-1, 0)]
    near += [cur_dev(0, 1, 0), cur_dev(1, 0, 0), cur_dev(-1, 0, 0), cur_dev(0, 0, 1)]
    for d in near:
        pl.semaphore_signal(barrier, inc=1, device_id=d, device_id_type=MESH)
    pl.semaphore_wait(barrier, len(near))

    ring = ((1, 0), (-1, 1))
    back = ((1, 1), (-1, 0))
    G_Y, G_OWN, G_FAR, G_P, G_LAST, G_CORE = 0, 2, 6, 8, 10, 12

    def core(slot, h, group):
        go(C.at[slot, 0, HALF[h]], C.at[slot, 1, HALF[h]], cur_dev(0, 0, 1), 1, G_CORE + group)

    def both(i_src, c_src, slot, h, d, y, recv):
        go(i_src, I.at[slot, HALF[h]], img_dev(d, y), 0, recv)
        go(c_src, C.at[slot, 0, HALF[h]], cur_dev(d, y, 0), 0, recv)

    def onward(slot, to, h, d, y, recv):
        both(I.at[slot, HALF[h]], C.at[slot, 0, HALF[h]], to, h, d, y, recv)

    def own_sem(d, h):
        return G_OWN + (d + 1) + h

    for h in range(2):
        both(img_ref.at[HALF[h]], cur_ref.at[HALF[h]], 1, h, 0, 1, G_Y + h)
        for d, k in ring if h == 0 else back:
            both(img_ref.at[HALF[k]], cur_ref.at[HALF[k]], SLOT[-d, 0], k, d, 0, own_sem(d, k))
    go(cur_ref, C.at[0, 1], cur_dev(0, 0, 1), 1, G_CORE)
    I[0] = img_ref[...]
    C[0, 0] = cur_ref[...]
    pos = jnp.sum(img_ref[...].astype(F32) * cur_ref[...].astype(F32), axis=1, keepdims=True) * gain
    pos = jnp.sum(pos, axis=0, keepdims=True)
    for d, h in ring:
        got(own_sem(d, h), I.at[0])
        onward(SLOT[-d, 0], SLOT[2, 0], h, d, 0, G_FAR + h)
        core(SLOT[-d, 0], h, 0)
    for h in range(2):
        got(G_Y + h, I.at[0])
        for d, k in ring if h == 0 else back:
            onward(1, SLOT[-d, 1], h, d, 0, G_P + h)
        core(1, h, 0)
        if h == 0:
            for d, k in back:
                got(own_sem(d, k), I.at[0])
                core(SLOT[-d, 0], k, 0)

    def scores(rows, cols):
        r0, r1 = rows

        def step(q, carry):
            a = I[r0:r1].reshape((r1 - r0) * 128, 1024)
            s = nt(a, C[q].reshape(256, 1024)) * gain
            S[q, r0:r1] = s.reshape(r1 - r0, 128, 256)
            return carry

        lax.fori_loop(cols[0], cols[1], step, 0)

    def row_stats(rows, cols, fresh):
        def step(a, carry):
            parts = [S[q, a, :, h * 128 : h * 128 + 128] for q in range(*cols) for h in range(2)]
            m = functools.reduce(jnp.maximum, parts)
            if fresh:
                total = functools.reduce(jnp.add, [jnp.exp(v - m) for v in parts])
            else:
                old = RM[a]
                m = jnp.maximum(m, old)
                total = RL[a] * jnp.exp(old - m)
                total = functools.reduce(jnp.add, [jnp.exp(v - m) for v in parts], total)
            RM[a] = m
            RL[a] = total
            return carry

        lax.fori_loop(rows[0], rows[1], step, 0)

    def col_stats(rows, cols, fresh):
        r0, r1 = rows

        def step(q, carry):
            s = S[q, r0:r1].reshape((r1 - r0) * 16, 8, 256)
            m = jnp.max(s, axis=0)
            if not fresh:
                old = CM[q]
                m = jnp.maximum(m, old)
            total = jnp.sum(jnp.exp(s - m[None]), axis=0)
            if not fresh:
                total = total + CL[q] * jnp.exp(old - m)
            CM[q] = m
            CL[q] = total
            return carry

        lax.fori_loop(cols[0], cols[1], step, 0)

    got(G_CORE, S.at[0])
    scores((0, 4), (0, 4))
    for h in range(2):
        got(G_FAR + h, I.at[0])
        onward(SLOT[2, 0], SLOT[2, 1], h, 0, 1, G_LAST + h)
        core(SLOT[2, 0], h, 1)
    row_stats((0, 4), (0, 4), True)
    col_stats((0, 4), (0, 4), True)
    for h in range(2):
        got(G_P + h, I.at[0:2])
        core(SLOT[1, 1], h, 1)
        core(SLOT[-1, 1], h, 1)
    got(G_CORE + 1, S.at[0, 0:6])
    scores((4, 7), (0, 4))
    scores((0, 7), (4, 7))
    row_stats((0, 4), (4, 7), False)
    row_stats((4, 7), (0, 7), True)
    col_stats((4, 7), (0, 4), False)
    col_stats((0, 7), (4, 7), True)
    for h in range(2):
        got(G_LAST + h, I.at[0])
        core(SLOT[2, 1], h, 2)
    scores((7, 8), (0, 7))
    got(G_CORE + 2, I.at[0])
    scores((0, 8), (7, 8))
    col_stats((7, 8), (0, 7), False)
    col_stats((0, 8), (7, 8), True)
    row_stats((0, 7), (7, 8), False)
    row_stats((7, 8), (0, 8), True)

    def img_place(dx, dy):
        return ((x + dx + 4) % 4) * 2 + (yl + dy) % 2

    def cur_place(dz, dy, dc):
        return ((c + dc) % 2) * 8 + ((z + dz + 4) % 4) * 2 + (yh + dy) % 2

    mi = img_place(0, 0)
    mc = cur_place(0, 0, 0)
    for q, (dz, dy) in enumerate(PLACES):
        m = CM[q]
        high = jnp.max(m, axis=0, keepdims=True)
        lse = high + jnp.log(jnp.sum(CL[q] * jnp.exp(m - high), axis=0, keepdims=True))
        cst[mc, pl.ds(cur_place(dz, dy, 0), 1), :] = lse[:, :128]
        cst[mc, pl.ds(cur_place(dz, dy, 1), 1), :] = lse[:, 128:]
    for d in cur_peers:
        go(cst.at[mc], cst.at[mc], cur_dev(*d), 2, 15)
    for a, (dx, dy) in enumerate(PLACES):
        m = RM[a].T
        high = jnp.max(m, axis=0, keepdims=True)
        lse = high + jnp.log(jnp.sum(RL[a].T * jnp.exp(m - high), axis=0, keepdims=True))
        rst[mi, pl.ds(img_place(dx, dy), 1), :] = lse
    rst[mi, 8:16, :] = jnp.broadcast_to(pos, (8, 128))
    for d in img_peers:
        go(rst.at[mi], rst.at[mi], img_dev(*d), 3, 16)
    got(16, rst.at[0:7])
    parts = [rst[k, 0:8, :] for k in range(8)]
    high = functools.reduce(jnp.maximum, parts)
    tot_r[...] = high + jnp.log(functools.reduce(jnp.add, [jnp.exp(v - high) for v in parts]))
    for a, (dx, dy) in enumerate(PLACES):
        RM[a] = jnp.broadcast_to(tot_r[pl.ds(img_place(dx, dy), 1), :], (128, 128)).T
    got(15, cst.at[0:15])
    parts = [cst[k] for k in range(16)]
    high = functools.reduce(jnp.maximum, parts)
    tot_c[...] = high + jnp.log(functools.reduce(jnp.add, [jnp.exp(v - high) for v in parts]))

    for q, (dz, dy) in enumerate(PLACES):
        for h in range(2):
            CM[q, :, h * 128 : h * 128 + 128] = jnp.broadcast_to(tot_c[pl.ds(cur_place(dz, dy, h), 1), :], (8, 128))

    def weigh(q, a):
        rl = RM[a]
        for h in range(2):
            lanes = slice(h * 128, h * 128 + 128)
            s = S[q, a, :, lanes]
            cl = CM[q, 0:1, lanes]
            W[q, a, :, lanes] = ((jnp.exp(s - rl) + jnp.exp(s - cl)) * 0.5).astype(BF16)

    def weights_by_row(rows, qs):
        def step(a, carry):
            for q in qs:
                weigh(q, a)
            return carry

        lax.fori_loop(rows[0], rows[1], step, 0)

    def weights_by_col(cols, rows):
        def step(q, carry):
            for a in rows:
                weigh(q, a)
            return carry

        lax.fori_loop(cols[0], cols[1], step, 0)

    R_SWAP = 17

    def curve_part(q):
        part = tn(W[q].reshape(1024, 256), I[...].reshape(1024, 1024))
        qo[q, 1] = part[128:256]
        go(qo.at[q, 1], qoin.at[q], cur_dev(0, 0, 1), 4, R_SWAP + q)
        qo[q, 0] = part[0:128]

    def joined(q):
        got(R_SWAP + q, qoin.at[q])
        return qo[q, 0] + qoin[q]

    def image_part(a1, a2):
        w = jnp.concatenate(
            [jnp.concatenate([W[q, a] for q in range(8)], axis=1) for a in (a1, a2)], axis=0
        )
        return nn(w, C[...].reshape(2048, 1024))

    class Side:
        def __init__(self, w, into, keep, far, own, last, base, send, to):
            self.w, self.into, self.keep, self.far, self.own, self.last = w, into, keep, far, own, last
            self.base, self.send, self.to = base, send, to

        def go(self, y, k, h, d, dy, recv):
            go(self.w.at[y, k, h], self.into.at[y, k, h], self.to(d, dy), self.send, self.base + recv)

        def across(self, part):
            self.w[1, 0] = part.astype(BF16)
            for h in range(2):
                self.go(1, 0, HALF[h], 0, 1, h)

        def straight(self, d, part):
            k = 1 if d == 1 else 2
            self.w[1, k] = part.astype(BF16)
            self.go(1, k, slice(0, 128), d, 0, 2)

        def two_steps(self):
            for d, h in ring:
                got(self.base + h, py.at[0, HALF[0]])
                self.w[0, 0, HALF[h]] = (self.far[HALF[h]] + self.into[1, 0, HALF[h]].astype(F32)).astype(BF16)
                self.go(0, 0, HALF[h], d, 0, 3 + h)

        def first_half(self, d, part):
            k, through = (1, 0) if d == 1 else (2, 1)
            rest = HALF[1 - through]
            self.w[0, k, rest] = part[rest].astype(BF16)
            self.go(0, k, rest, d, 0, 5)
            self.keep[k - 1] = part[HALF[through]]

        def second_half(self):
            for d, h in ring:
                k = 1 if d == 1 else 2
                got(self.base + 3 + h, py.at[0, HALF[0]])
                self.w[0, k, HALF[h]] = (self.keep[k - 1] + self.into[0, 0, HALF[h]].astype(F32)).astype(BF16)
                self.go(0, k, HALF[h], d, 0, 5)

        def finish_partner(self):
            got(self.base + 2, I.at[0:2])
            self.last[0] = (self.own[1] + self.into[1, 1].astype(F32) + self.into[1, 2].astype(F32)).astype(BF16)
            go(self.last.at[0], self.last.at[1], self.to(0, 1), self.send, self.base + 6)

        def finish_own(self, other):
            got(self.base + 5, I.at[0:2])
            self.own[0] = self.own[0] + self.into[0, 1].astype(F32) + self.into[0, 2].astype(F32) - other

        def result(self):
            got(self.base + 6, I.at[0])
            return (self.own[0] + self.last[1].astype(F32)) * gain

    img = Side(pw, pin, pf, pa, pown, py, 25, 5, img_dev)
    cur = Side(qw, qin, qf, qa, qown, qy, 32, 5, lambda d, dy: cur_dev(d, dy, 0))

    weights_by_row((0, 8), (7,))
    curve_part(SLOT[2, 1])
    weights_by_col((0, 7), (4, 7))
    part = image_part(SLOT[2, 1], SLOT[2, 0])
    img.across(part[0:128])
    pa[...] = part[128:256]
    cur.across(joined(SLOT[2, 1]))
    weights_by_row((0, 4), (5, 6))
    weights_by_row((5, 7), (5, 6))
    curve_part(SLOT[1, 1])
    curve_part(SLOT[-1, 1])
    weights_by_col((0, 5), (5, 6))
    part = image_part(SLOT[1, 1], SLOT[-1, 1])
    img.straight(1, part[0:128])
    img.straight(-1, part[128:256])
    cur.straight(1, joined(SLOT[1, 1]))
    cur.straight(-1, joined(SLOT[-1, 1]))
    weights_by_col((0, 5), (0, 1, 2, 3))
    curve_part(SLOT[2, 0])
    curve_part(SLOT[1, 0])
    curve_part(SLOT[-1, 0])
    part = image_part(SLOT[1, 0], SLOT[-1, 0])
    img.two_steps()
    qa[...] = joined(SLOT[2, 0])
    cur.two_steps()
    img.first_half(1, part[0:128])
    img.first_half(-1, part[128:256])
    cur.first_half(1, joined(SLOT[1, 0]))
    cur.first_half(-1, joined(SLOT[-1, 0]))
    curve_part(SLOT[0, 1])
    curve_part(SLOT[0, 0])
    part = image_part(SLOT[0, 1], SLOT[0, 0])
    pown[1] = part[0:128]
    pown[0] = part[128:256]
    qown[1] = joined(SLOT[0, 1])
    qown[0] = joined(SLOT[0, 0])
    img.finish_partner()
    cur.finish_partner()
    img.second_half()
    cur.second_half()

    def grand(v):
        return jnp.sum(jnp.sum(v, axis=1, keepdims=True), axis=0, keepdims=True)

    pos_all = functools.reduce(jnp.add, [rst[k, 8:16, :] for k in range(8)])
    val_c[mc] = grand(tot_r[...]) - 2.0 * pos_all
    val_r[mi] = jnp.broadcast_to(grand(tot_c[...]), (8, 128))
    for d in cur_peers:
        go(val_c.at[mc], val_c.at[mc], cur_dev(*d), 6, 39)
    for d in img_peers:
        go(val_r.at[mi], val_r.at[mi], img_dev(*d), 7, 40)

    img.finish_own(cur_ref[...].astype(F32))
    cur.finish_own(img_ref[...].astype(F32))
    got(39, val_c.at[0:15])
    got(40, val_r.at[0:7])
    total = sum(val_c[k] for k in range(16)) + sum(val_r[k] for k in range(8))
    loss_ref[...] = total[0:1, 0:1] / (2.0 * pairs)
    dimg_ref[...] = img.result()
    dcur_ref[...] = cur.result()
    left(0, S.at[0:4, 0:7])
    left(1, S.at[0:2])
    left(2, cst.at[0:15])
    left(3, rst.at[0:7])
    left(4, S.at[0:4])
    left(5, S.at[0:4, 0:7])
    left(6, val_c.at[0:15])
    left(7, val_r.at[0:7])


def solution(mesh):
    def step(image_emb, curve_emb):
        gain = math.sqrt(image_emb.shape[1])
        vmem = pl.BlockSpec(memory_space=pltpu.VMEM)
        loss, dimg, dcur = pl.pallas_call(
            functools.partial(kernel, gain, 16384),
            out_shape=(
                jax.ShapeDtypeStruct((1, 1), F32),
                jax.ShapeDtypeStruct((128, 1024), F32),
                jax.ShapeDtypeStruct((128, 1024), F32),
            ),
            in_specs=[vmem, vmem],
            out_specs=(vmem, vmem, vmem),
            scratch_shapes=[
                pltpu.VMEM((8, 128, 1024), BF16),
                pltpu.VMEM((8, 2, 128, 1024), BF16),
                pltpu.VMEM((8, 8, 128, 256), F32),
                pltpu.VMEM((8, 8, 128, 256), BF16),
                pltpu.VMEM((8, 128, 128), F32),
                pltpu.VMEM((8, 128, 128), F32),
                pltpu.VMEM((8, 8, 256), F32),
                pltpu.VMEM((8, 8, 256), F32),
                pltpu.VMEM((8, 16, 128), F32),
                pltpu.VMEM((16, 16, 128), F32),
                pltpu.VMEM((8, 128), F32),
                pltpu.VMEM((16, 128), F32),
                pltpu.VMEM((8, 8, 128), F32),
                pltpu.VMEM((16, 8, 128), F32),
                pltpu.VMEM((2, 3, 128, 1024), BF16),
                pltpu.VMEM((2, 3, 128, 1024), BF16),
                pltpu.VMEM((2, 64, 1024), F32),
                pltpu.VMEM((128, 1024), F32),
                pltpu.VMEM((2, 128, 1024), F32),
                pltpu.VMEM((2, 128, 1024), BF16),
                pltpu.VMEM((8, 2, 128, 1024), F32),
                pltpu.VMEM((8, 128, 1024), F32),
                pltpu.VMEM((2, 3, 128, 1024), BF16),
                pltpu.VMEM((2, 3, 128, 1024), BF16),
                pltpu.VMEM((2, 64, 1024), F32),
                pltpu.VMEM((128, 1024), F32),
                pltpu.VMEM((2, 128, 1024), F32),
                pltpu.VMEM((2, 128, 1024), BF16),
                pltpu.SemaphoreType.DMA((8,)),
                pltpu.SemaphoreType.DMA((41,)),
            ],
            compiler_params=pltpu.CompilerParams(
                collective_id=0, has_side_effects=True, vmem_limit_bytes=48 << 20
            ),
        )(image_emb, curve_emb)
        return loss.reshape(()), dimg, dcur

    spec = P(("blk", "rep"), None)
    return jax.shard_map(step, mesh=mesh, in_specs=(spec, spec), out_specs=(P(), spec, spec), check_vma=False)
```

```python
import functools
import math

import jax
import jax.numpy as jnp
from jax import lax
from jax.experimental import pallas as pl
from jax.experimental.pallas import tpu as pltpu
from jax.sharding import PartitionSpec as P

F32, BF16 = jnp.float32, jnp.bfloat16
MESH = pl.DeviceIdType.MESH
PLACES = ((0, 0), (0, 1), (-1, 0), (1, 0), (2, 0), (-1, 1), (1, 1), (2, 1))
SLOT = {p: k for k, p in enumerate(PLACES)}
HALF = (slice(0, 64), slice(64, 128))


def nt(a, b):
    return lax.dot_general(a, b, (((1,), (1,)), ((), ())), preferred_element_type=F32)


def nn(a, b):
    return lax.dot_general(a, b, (((1,), (0,)), ((), ())), preferred_element_type=F32)


def tn(a, b):
    return lax.dot_general(a, b, (((0,), (0,)), ((), ())), preferred_element_type=F32)


def kernel(
    gain,
    pairs,
    img_ref,
    cur_ref,
    loss_ref,
    dimg_ref,
    dcur_ref,
    I,
    C,
    S,
    W,
    RM,
    RL,
    CM,
    CL,
    rst,
    cst,
    tot_r,
    tot_c,
    val_r,
    val_c,
    pw,
    pin,
    pf,
    pa,
    pown,
    py,
    qo,
    qoin,
    qw,
    qin,
    qf,
    qa,
    qown,
    qy,
    sends,
    recvs,
    locals_,
):
    blk, rep = lax.axis_index("blk"), lax.axis_index("rep")
    x = blk % 4
    z = (blk // 4) % 4
    yh = blk // 16
    yl = rep // 2
    c = rep % 2

    def dev(x, yl, z, yh, c):
        return ((yh * 4 + z) * 4 + x, yl * 2 + c)

    def img_dev(dx, dy):
        return dev((x + dx + 4) % 4, (yl + dy) % 2, z, yh, c)

    def cur_dev(dz, dy, dc):
        return dev(x, (yl + dy) % 2, (z + dz + 4) % 4, (yh + dy) % 2, (c + dc) % 2)

    def go(src, dst, device, send, recv):
        pltpu.make_async_remote_copy(
            src_ref=src,
            dst_ref=dst,
            send_sem=sends.at[send],
            recv_sem=recvs.at[recv],
            device_id=device,
            device_id_type=MESH,
        ).start()

    def got(recv, size):
        pltpu.make_async_copy(size, size, recvs.at[recv]).wait()

    def left(send, size):
        pltpu.make_async_copy(size, size, sends.at[send]).wait()

    load_i = pltpu.make_async_copy(img_ref, I.at[0], locals_.at[0])
    load_c = pltpu.make_async_copy(cur_ref, C.at[0, 0], locals_.at[1])
    load_i.start()
    load_c.start()

    img_peers = [(dx, dy) for dx in range(4) for dy in range(2) if dx or dy]
    cur_peers = [(dz, dy, dc) for dz in range(4) for dy in range(2) for dc in range(2) if dz or dy or dc]

    barrier = pltpu.get_barrier_semaphore()
    near = [img_dev(0, 1), img_dev(1, 0), img_dev(-1, 0)]
    near += [cur_dev(0, 1, 0), cur_dev(1, 0, 0), cur_dev(-1, 0, 0), cur_dev(0, 0, 1)]
    for d in near:
        pl.semaphore_signal(barrier, inc=1, device_id=d, device_id_type=MESH)
    load_i.wait()
    load_c.wait()
    pl.semaphore_wait(barrier, len(near))

    ring = ((1, 0), (-1, 1))
    back = ((1, 1), (-1, 0))
    G_Y, G_OWN, G_FAR, G_P, G_LAST, G_CORE = 0, 2, 6, 8, 10, 12

    def core(slot, h, group):
        go(C.at[slot, 0, HALF[h]], C.at[slot, 1, HALF[h]], cur_dev(0, 0, 1), 1, G_CORE + group)

    def both(i_src, c_src, slot, h, d, y, recv):
        go(i_src, I.at[slot, HALF[h]], img_dev(d, y), 0, recv)
        go(c_src, C.at[slot, 0, HALF[h]], cur_dev(d, y, 0), 0, recv)

    def onward(slot, to, h, d, y, recv):
        both(I.at[slot, HALF[h]], C.at[slot, 0, HALF[h]], to, h, d, y, recv)

    def own_sem(d, h):
        return G_OWN + (d + 1) + h

    for h in range(2):
        both(I.at[0, HALF[h]], C.at[0, 0, HALF[h]], 1, h, 0, 1, G_Y + h)
        for d, k in ring if h == 0 else back:
            both(I.at[0, HALF[k]], C.at[0, 0, HALF[k]], SLOT[-d, 0], k, d, 0, own_sem(d, k))
    go(C.at[0, 0], C.at[0, 1], cur_dev(0, 0, 1), 1, G_CORE)
    pos = jnp.sum(I[0].astype(F32) * C[0, 0].astype(F32), axis=1, keepdims=True) * gain
    pos = jnp.sum(pos, axis=0, keepdims=True)
    for d, h in ring:
        got(own_sem(d, h), I.at[0])
        onward(SLOT[-d, 0], SLOT[2, 0], h, d, 0, G_FAR + h)
        core(SLOT[-d, 0], h, 0)
    for h in range(2):
        got(G_Y + h, I.at[0])
        for d, k in ring if h == 0 else back:
            onward(1, SLOT[-d, 1], h, d, 0, G_P + h)
        core(1, h, 0)
        if h == 0:
            for d, k in back:
                got(own_sem(d, k), I.at[0])
                core(SLOT[-d, 0], k, 0)

    def scores(rows, cols):
        r0, r1 = rows

        def some(q, n):
            a = I[r0:r1].reshape((r1 - r0) * 128, 1024)
            s = nt(a, C[pl.ds(q, n)].reshape(n * 256, 1024)) * gain
            for k in range(n):
                S[q + k, r0:r1] = s[:, k * 256 : k * 256 + 256].reshape(r1 - r0, 128, 256)

        for q in range(cols[0], cols[1], 4):
            some(q, min(4, cols[1] - q))

    def row_stats(rows, cols, fresh):
        def step(a, carry):
            parts = [S[q, a, :, h * 128 : h * 128 + 128] for q in range(*cols) for h in range(2)]
            m = functools.reduce(jnp.maximum, parts)
            if fresh:
                total = functools.reduce(jnp.add, [jnp.exp(v - m) for v in parts])
            else:
                old = RM[a]
                m = jnp.maximum(m, old)
                total = RL[a] * jnp.exp(old - m)
                total = functools.reduce(jnp.add, [jnp.exp(v - m) for v in parts], total)
            RM[a] = m
            RL[a] = total
            return carry

        lax.fori_loop(rows[0], rows[1], step, 0)

    def col_stats(rows, cols, fresh):
        r0, r1 = rows

        def step(q, carry):
            s = S[q, r0:r1].reshape((r1 - r0) * 16, 8, 256)
            m = jnp.max(s, axis=0)
            if not fresh:
                old = CM[q]
                m = jnp.maximum(m, old)
            total = jnp.sum(jnp.exp(s - m[None]), axis=0)
            if not fresh:
                total = total + CL[q] * jnp.exp(old - m)
            CM[q] = m
            CL[q] = total
            return carry

        lax.fori_loop(cols[0], cols[1], step, 0)

    got(G_CORE, S.at[0])
    scores((0, 4), (0, 4))
    for h in range(2):
        got(G_FAR + h, I.at[0])
        onward(SLOT[2, 0], SLOT[2, 1], h, 0, 1, G_LAST + h)
        core(SLOT[2, 0], h, 1)
    row_stats((0, 4), (0, 4), True)
    col_stats((0, 4), (0, 4), True)
    got(G_CORE + 1, I.at[0])
    scores((4, 5), (0, 4))
    scores((0, 5), (4, 5))
    for h in range(2):
        got(G_P + h, I.at[0:2])
        core(SLOT[1, 1], h, 2)
        core(SLOT[-1, 1], h, 2)
    got(G_CORE + 2, I.at[0:2])
    scores((5, 7), (0, 5))
    scores((0, 7), (5, 7))
    row_stats((0, 4), (4, 7), False)
    row_stats((4, 7), (0, 7), True)
    col_stats((4, 7), (0, 4), False)
    col_stats((0, 7), (4, 7), True)
    for h in range(2):
        got(G_LAST + h, I.at[0])
        core(SLOT[2, 1], h, 3)
    scores((7, 8), (0, 7))
    got(G_CORE + 3, I.at[0])
    scores((0, 8), (7, 8))
    col_stats((7, 8), (0, 7), False)
    col_stats((0, 8), (7, 8), True)
    row_stats((0, 7), (7, 8), False)
    row_stats((7, 8), (0, 8), True)

    def img_place(dx, dy):
        return ((x + dx + 4) % 4) * 2 + (yl + dy) % 2

    def cur_place(dz, dy, dc):
        return ((c + dc) % 2) * 8 + ((z + dz + 4) % 4) * 2 + (yh + dy) % 2

    mi = img_place(0, 0)
    mc = cur_place(0, 0, 0)
    for q, (dz, dy) in enumerate(PLACES):
        m = CM[q]
        high = jnp.max(m, axis=0, keepdims=True)
        lse = high + jnp.log(jnp.sum(CL[q] * jnp.exp(m - high), axis=0, keepdims=True))
        cst[mc, pl.ds(cur_place(dz, dy, 0), 1), :] = lse[:, :128]
        cst[mc, pl.ds(cur_place(dz, dy, 1), 1), :] = lse[:, 128:]
    for d in cur_peers:
        go(cst.at[mc], cst.at[mc], cur_dev(*d), 2, 16)
    for a, (dx, dy) in enumerate(PLACES):
        m = RM[a].T
        high = jnp.max(m, axis=0, keepdims=True)
        lse = high + jnp.log(jnp.sum(RL[a].T * jnp.exp(m - high), axis=0, keepdims=True))
        rst[mi, pl.ds(img_place(dx, dy), 1), :] = lse
    rst[mi, 8:16, :] = jnp.broadcast_to(pos, (8, 128))
    for d in img_peers:
        go(rst.at[mi], rst.at[mi], img_dev(*d), 3, 17)
    got(17, rst.at[0:7])
    parts = [rst[k, 0:8, :] for k in range(8)]
    high = functools.reduce(jnp.maximum, parts)
    tot_r[...] = high + jnp.log(functools.reduce(jnp.add, [jnp.exp(v - high) for v in parts]))
    for a, (dx, dy) in enumerate(PLACES):
        RM[a] = jnp.broadcast_to(tot_r[pl.ds(img_place(dx, dy), 1), :], (128, 128)).T
    got(16, cst.at[0:15])
    parts = [cst[k] for k in range(16)]
    high = functools.reduce(jnp.maximum, parts)
    tot_c[...] = high + jnp.log(functools.reduce(jnp.add, [jnp.exp(v - high) for v in parts]))

    for q, (dz, dy) in enumerate(PLACES):
        for h in range(2):
            CM[q, :, h * 128 : h * 128 + 128] = jnp.broadcast_to(tot_c[pl.ds(cur_place(dz, dy, h), 1), :], (8, 128))

    def weigh(q, a):
        rl = RM[a]
        for h in range(2):
            lanes = slice(h * 128, h * 128 + 128)
            s = S[q, a, :, lanes]
            cl = CM[q, 0:1, lanes]
            W[q, a, :, lanes] = ((jnp.exp(s - rl) + jnp.exp(s - cl)) * 0.5).astype(BF16)

    def weights_by_row(rows, qs):
        def step(a, carry):
            for q in qs:
                weigh(q, a)
            return carry

        lax.fori_loop(rows[0], rows[1], step, 0)

    def weights_by_col(cols, rows):
        def step(q, carry):
            for a in rows:
                weigh(q, a)
            return carry

        lax.fori_loop(cols[0], cols[1], step, 0)

    R_SWAP = 18

    def curve_part(q):
        part = tn(W[q].reshape(1024, 256), I[...].reshape(1024, 1024))
        qo[q, 1] = part[128:256]
        go(qo.at[q, 1], qoin.at[q], cur_dev(0, 0, 1), 4, R_SWAP + q)
        qo[q, 0] = part[0:128]

    def joined(q):
        got(R_SWAP + q, qoin.at[q])
        return qo[q, 0] + qoin[q]

    def image_part(a1, a2):
        w = jnp.concatenate(
            [jnp.concatenate([W[q, a] for q in range(8)], axis=1) for a in (a1, a2)], axis=0
        )
        return nn(w, C[...].reshape(2048, 1024))

    class Side:
        def __init__(self, w, into, keep, far, own, last, base, send, to):
            self.w, self.into, self.keep, self.far, self.own, self.last = w, into, keep, far, own, last
            self.base, self.send, self.to = base, send, to

        def go(self, y, k, h, d, dy, recv):
            go(self.w.at[y, k, h], self.into.at[y, k, h], self.to(d, dy), self.send, self.base + recv)

        def across(self, part):
            self.w[1, 0] = part.astype(BF16)
            for h in range(2):
                self.go(1, 0, HALF[h], 0, 1, h)

        def straight(self, d, part):
            k = 1 if d == 1 else 2
            self.w[1, k] = part.astype(BF16)
            self.go(1, k, slice(0, 128), d, 0, 2)

        def two_steps(self):
            for d, h in ring:
                got(self.base + h, py.at[0, HALF[0]])
                self.w[0, 0, HALF[h]] = (self.far[HALF[h]] + self.into[1, 0, HALF[h]].astype(F32)).astype(BF16)
                self.go(0, 0, HALF[h], d, 0, 3 + h)

        def first_half(self, d, part):
            k, through = (1, 0) if d == 1 else (2, 1)
            rest = HALF[1 - through]
            self.w[0, k, rest] = part[rest].astype(BF16)
            self.go(0, k, rest, d, 0, 5)
            self.keep[k - 1] = part[HALF[through]]

        def second_half(self):
            for d, h in ring:
                k = 1 if d == 1 else 2
                got(self.base + 3 + h, py.at[0, HALF[0]])
                self.w[0, k, HALF[h]] = (self.keep[k - 1] + self.into[0, 0, HALF[h]].astype(F32)).astype(BF16)
                self.go(0, k, HALF[h], d, 0, 5)

        def finish_partner(self):
            got(self.base + 2, I.at[0:2])
            self.last[0] = (self.own[1] + self.into[1, 1].astype(F32) + self.into[1, 2].astype(F32)).astype(BF16)
            go(self.last.at[0], self.last.at[1], self.to(0, 1), self.send, self.base + 6)

        def finish_own(self, other):
            got(self.base + 5, I.at[0:2])
            self.own[0] = self.own[0] + self.into[0, 1].astype(F32) + self.into[0, 2].astype(F32) - other

        def result(self):
            got(self.base + 6, I.at[0])
            return (self.own[0] + self.last[1].astype(F32)) * gain

    img = Side(pw, pin, pf, pa, pown, py, 26, 5, img_dev)
    cur = Side(qw, qin, qf, qa, qown, qy, 33, 5, lambda d, dy: cur_dev(d, dy, 0))

    weights_by_row((0, 8), (7,))
    curve_part(SLOT[2, 1])
    weights_by_col((0, 7), (4, 7))
    part = image_part(SLOT[2, 1], SLOT[2, 0])
    img.across(part[0:128])
    pa[...] = part[128:256]
    cur.across(joined(SLOT[2, 1]))
    weights_by_row((0, 4), (5, 6))
    weights_by_row((5, 7), (5, 6))
    curve_part(SLOT[1, 1])
    curve_part(SLOT[-1, 1])
    weights_by_col((0, 5), (5, 6))
    part = image_part(SLOT[1, 1], SLOT[-1, 1])
    img.straight(1, part[0:128])
    img.straight(-1, part[128:256])
    cur.straight(1, joined(SLOT[1, 1]))
    cur.straight(-1, joined(SLOT[-1, 1]))
    weights_by_col((0, 5), (0, 1, 2, 3))
    curve_part(SLOT[2, 0])
    curve_part(SLOT[1, 0])
    curve_part(SLOT[-1, 0])
    part = image_part(SLOT[1, 0], SLOT[-1, 0])
    img.two_steps()
    qa[...] = joined(SLOT[2, 0])
    cur.two_steps()
    img.first_half(1, part[0:128])
    img.first_half(-1, part[128:256])
    cur.first_half(1, joined(SLOT[1, 0]))
    cur.first_half(-1, joined(SLOT[-1, 0]))
    curve_part(SLOT[0, 1])
    curve_part(SLOT[0, 0])
    part = image_part(SLOT[0, 1], SLOT[0, 0])
    pown[1] = part[0:128]
    pown[0] = part[128:256]
    qown[1] = joined(SLOT[0, 1])
    qown[0] = joined(SLOT[0, 0])
    img.finish_partner()
    cur.finish_partner()
    img.second_half()
    cur.second_half()

    def grand(v):
        return jnp.sum(jnp.sum(v, axis=1, keepdims=True), axis=0, keepdims=True)

    pos_all = functools.reduce(jnp.add, [rst[k, 8:16, :] for k in range(8)])
    val_c[mc] = grand(tot_r[...]) - 2.0 * pos_all
    val_r[mi] = jnp.broadcast_to(grand(tot_c[...]), (8, 128))
    for d in cur_peers:
        go(val_c.at[mc], val_c.at[mc], cur_dev(*d), 6, 40)
    for d in img_peers:
        go(val_r.at[mi], val_r.at[mi], img_dev(*d), 7, 41)

    img.finish_own(C[0, 0].astype(F32))
    cur.finish_own(I[0].astype(F32))
    got(40, val_c.at[0:15])
    got(41, val_r.at[0:7])
    total = sum(val_c[k] for k in range(16)) + sum(val_r[k] for k in range(8))
    loss_ref[...] = total[0:1, 0:1] / (2.0 * pairs)
    dimg_ref[...] = img.result()
    dcur_ref[...] = cur.result()
    left(0, S.at[0:4, 0:7])
    left(1, S.at[0:2])
    left(2, cst.at[0:15])
    left(3, rst.at[0:7])
    left(4, S.at[0:4])
    left(5, S.at[0:4, 0:7])
    left(6, val_c.at[0:15])
    left(7, val_r.at[0:7])


def solution(mesh):
    def step(image_emb, curve_emb):
        gain = math.sqrt(image_emb.shape[1])
        vmem = pl.BlockSpec(memory_space=pltpu.VMEM)
        loss, dimg, dcur = pl.pallas_call(
            functools.partial(kernel, gain, 16384),
            out_shape=(
                jax.ShapeDtypeStruct((1, 1), F32),
                jax.ShapeDtypeStruct((128, 1024), F32),
                jax.ShapeDtypeStruct((128, 1024), F32),
            ),
            in_specs=[pl.BlockSpec(memory_space=pltpu.HBM)] * 2,
            out_specs=(vmem, vmem, vmem),
            scratch_shapes=[
                pltpu.VMEM((8, 128, 1024), BF16),
                pltpu.VMEM((8, 2, 128, 1024), BF16),
                pltpu.VMEM((8, 8, 128, 256), F32),
                pltpu.VMEM((8, 8, 128, 256), BF16),
                pltpu.VMEM((8, 128, 128), F32),
                pltpu.VMEM((8, 128, 128), F32),
                pltpu.VMEM((8, 8, 256), F32),
                pltpu.VMEM((8, 8, 256), F32),
                pltpu.VMEM((8, 16, 128), F32),
                pltpu.VMEM((16, 16, 128), F32),
                pltpu.VMEM((8, 128), F32),
                pltpu.VMEM((16, 128), F32),
                pltpu.VMEM((8, 8, 128), F32),
                pltpu.VMEM((16, 8, 128), F32),
                pltpu.VMEM((2, 3, 128, 1024), BF16),
                pltpu.VMEM((2, 3, 128, 1024), BF16),
                pltpu.VMEM((2, 64, 1024), F32),
                pltpu.VMEM((128, 1024), F32),
                pltpu.VMEM((2, 128, 1024), F32),
                pltpu.VMEM((2, 128, 1024), BF16),
                pltpu.VMEM((8, 2, 128, 1024), F32),
                pltpu.VMEM((8, 128, 1024), F32),
                pltpu.VMEM((2, 3, 128, 1024), BF16),
                pltpu.VMEM((2, 3, 128, 1024), BF16),
                pltpu.VMEM((2, 64, 1024), F32),
                pltpu.VMEM((128, 1024), F32),
                pltpu.VMEM((2, 128, 1024), F32),
                pltpu.VMEM((2, 128, 1024), BF16),
                pltpu.SemaphoreType.DMA((8,)),
                pltpu.SemaphoreType.DMA((42,)),
                pltpu.SemaphoreType.DMA((2,)),
            ],
            compiler_params=pltpu.CompilerParams(
                collective_id=0, has_side_effects=True, vmem_limit_bytes=57 << 20
            ),
        )(image_emb, curve_emb)
        return loss.reshape(()), dimg, dcur

    spec = P(("blk", "rep"), None)
    return jax.shard_map(step, mesh=mesh, in_specs=(spec, spec), out_specs=(P(), spec, spec), check_vma=False)
```

```python
import functools
import math

import jax
import jax.numpy as jnp
from jax import lax
from jax.experimental import pallas as pl
from jax.experimental.pallas import tpu as pltpu
from jax.sharding import PartitionSpec as P

F32, BF16 = jnp.float32, jnp.bfloat16
MESH = pl.DeviceIdType.MESH
PLACES = ((0, 0), (0, 1), (-1, 0), (1, 0), (2, 0), (-1, 1), (1, 1), (2, 1))
SLOT = {p: k for k, p in enumerate(PLACES)}
HALF = (slice(0, 64), slice(64, 128))


def nt(a, b):
    return lax.dot_general(a, b, (((1,), (1,)), ((), ())), preferred_element_type=F32)


def nn(a, b):
    return lax.dot_general(a, b, (((1,), (0,)), ((), ())), preferred_element_type=F32)


def tn(a, b):
    return lax.dot_general(a, b, (((0,), (0,)), ((), ())), preferred_element_type=F32)


def kernel(
    gain,
    pairs,
    img_ref,
    cur_ref,
    loss_ref,
    dimg_ref,
    dcur_ref,
    I,
    C,
    S,
    W,
    RM,
    RL,
    CM,
    CL,
    rst,
    cst,
    tot_r,
    tot_c,
    val_r,
    val_c,
    pw,
    pin,
    pf,
    pa,
    pown,
    py,
    qo,
    qoin,
    qw,
    qin,
    qf,
    qa,
    qown,
    qy,
    sends,
    recvs,
    locals_,
):
    blk, rep = lax.axis_index("blk"), lax.axis_index("rep")
    x = blk % 4
    z = (blk // 4) % 4
    yh = blk // 16
    yl = rep // 2
    c = rep % 2

    def dev(x, yl, z, yh, c):
        return ((yh * 4 + z) * 4 + x, yl * 2 + c)

    def img_dev(dx, dy):
        return dev((x + dx + 4) % 4, (yl + dy) % 2, z, yh, c)

    def cur_dev(dz, dy, dc):
        return dev(x, (yl + dy) % 2, (z + dz + 4) % 4, (yh + dy) % 2, (c + dc) % 2)

    def go(src, dst, device, send, recv):
        pltpu.make_async_remote_copy(
            src_ref=src,
            dst_ref=dst,
            send_sem=sends.at[send],
            recv_sem=recvs.at[recv],
            device_id=device,
            device_id_type=MESH,
        ).start()

    def got(recv, size):
        pltpu.make_async_copy(size, size, recvs.at[recv]).wait()

    def left(send, size):
        pltpu.make_async_copy(size, size, sends.at[send]).wait()

    load_i = pltpu.make_async_copy(img_ref, I.at[0], locals_.at[0])
    load_c = pltpu.make_async_copy(cur_ref, C.at[0, 0], locals_.at[1])
    load_i.start()
    load_c.start()

    img_peers = [(dx, dy) for dx in range(4) for dy in range(2) if dx or dy]
    cur_peers = [(dz, dy, dc) for dz in range(4) for dy in range(2) for dc in range(2) if dz or dy or dc]

    barrier = pltpu.get_barrier_semaphore()
    near = [img_dev(0, 1), img_dev(1, 0), img_dev(-1, 0)]
    near += [cur_dev(0, 1, 0), cur_dev(1, 0, 0), cur_dev(-1, 0, 0), cur_dev(0, 0, 1)]
    for d in near:
        pl.semaphore_signal(barrier, inc=1, device_id=d, device_id_type=MESH)
    load_i.wait()
    load_c.wait()
    pl.semaphore_wait(barrier, len(near))

    ring = ((1, 0), (-1, 1))
    back = ((1, 1), (-1, 0))
    G_Y, G_OWN, G_FAR, G_P, G_LAST, G_CORE = 0, 2, 6, 8, 10, 12

    def core(slot, h, group):
        go(C.at[slot, 0, HALF[h]], C.at[slot, 1, HALF[h]], cur_dev(0, 0, 1), 1, G_CORE + group)

    def both(i_src, c_src, slot, h, d, y, recv):
        go(i_src, I.at[slot, HALF[h]], img_dev(d, y), 0, recv)
        go(c_src, C.at[slot, 0, HALF[h]], cur_dev(d, y, 0), 0, recv)

    def onward(slot, to, h, d, y, recv):
        both(I.at[slot, HALF[h]], C.at[slot, 0, HALF[h]], to, h, d, y, recv)

    def own_sem(d, h):
        return G_OWN + (d + 1) + h

    for h in range(2):
        both(I.at[0, HALF[h]], C.at[0, 0, HALF[h]], 1, h, 0, 1, G_Y + h)
        for d, k in ring if h == 0 else back:
            both(I.at[0, HALF[k]], C.at[0, 0, HALF[k]], SLOT[-d, 0], k, d, 0, own_sem(d, k))
    go(C.at[0, 0], C.at[0, 1], cur_dev(0, 0, 1), 1, G_CORE)
    pos = jnp.sum(I[0].astype(F32) * C[0, 0].astype(F32), axis=1, keepdims=True) * gain
    pos = jnp.sum(pos, axis=0, keepdims=True)
    for d, h in ring:
        got(own_sem(d, h), I.at[0])
        onward(SLOT[-d, 0], SLOT[2, 0], h, d, 0, G_FAR + h)
        core(SLOT[-d, 0], h, 0)
    for h in range(2):
        got(G_Y + h, I.at[0])
        for d, k in ring if h == 0 else back:
            onward(1, SLOT[-d, 1], h, d, 0, G_P + h)
        core(1, h, 0)
        if h == 0:
            for d, k in back:
                got(own_sem(d, k), I.at[0])
                core(SLOT[-d, 0], k, 0)

    def scores(rows, cols):
        r0, r1 = rows

        def some(q, n):
            a = I[r0:r1].reshape((r1 - r0) * 128, 1024)
            s = nt(a, C[pl.ds(q, n)].reshape(n * 256, 1024)) * gain
            for k in range(n):
                S[q + k, r0:r1] = s[:, k * 256 : k * 256 + 256].reshape(r1 - r0, 128, 256)

        for q in range(cols[0], cols[1], 4):
            some(q, min(4, cols[1] - q))

    def row_stats(rows, cols, fresh):
        def step(a, carry):
            parts = [S[q, a, :, h * 128 : h * 128 + 128] for q in range(*cols) for h in range(2)]
            m = functools.reduce(jnp.maximum, parts)
            if fresh:
                total = functools.reduce(jnp.add, [jnp.exp(v - m) for v in parts])
            else:
                old = RM[a]
                m = jnp.maximum(m, old)
                total = RL[a] * jnp.exp(old - m)
                total = functools.reduce(jnp.add, [jnp.exp(v - m) for v in parts], total)
            RM[a] = m
            RL[a] = total
            return carry

        lax.fori_loop(rows[0], rows[1], step, 0)

    def col_stats(rows, cols, fresh):
        r0, r1 = rows

        def step(q, carry):
            s = S[q, r0:r1].reshape((r1 - r0) * 16, 8, 256)
            m = jnp.max(s, axis=0)
            if not fresh:
                old = CM[q]
                m = jnp.maximum(m, old)
            total = jnp.sum(jnp.exp(s - m[None]), axis=0)
            if not fresh:
                total = total + CL[q] * jnp.exp(old - m)
            CM[q] = m
            CL[q] = total
            return carry

        lax.fori_loop(cols[0], cols[1], step, 0)

    for h in range(2):
        got(G_FAR + h, I.at[0])
        onward(SLOT[2, 0], SLOT[2, 1], h, 0, 1, G_LAST + h)
        core(SLOT[2, 0], h, 1)
    got(G_CORE, S.at[0])
    scores((0, 4), (0, 4))
    row_stats((0, 4), (0, 4), True)
    col_stats((0, 4), (0, 4), True)
    got(G_CORE + 1, I.at[0])
    scores((4, 5), (0, 4))
    scores((0, 5), (4, 5))
    for h in range(2):
        got(G_P + h, I.at[0:2])
        core(SLOT[1, 1], h, 2)
        core(SLOT[-1, 1], h, 2)
    got(G_CORE + 2, I.at[0:2])
    scores((5, 7), (0, 5))
    scores((0, 7), (5, 7))
    row_stats((0, 4), (4, 7), False)
    row_stats((4, 7), (0, 7), True)
    col_stats((4, 7), (0, 4), False)
    col_stats((0, 7), (4, 7), True)
    for h in range(2):
        got(G_LAST + h, I.at[0])
        core(SLOT[2, 1], h, 3)
    scores((7, 8), (0, 7))
    got(G_CORE + 3, I.at[0])
    scores((0, 8), (7, 8))
    col_stats((7, 8), (0, 7), False)
    col_stats((0, 8), (7, 8), True)
    row_stats((0, 7), (7, 8), False)
    row_stats((7, 8), (0, 8), True)

    def img_place(dx, dy):
        return ((x + dx + 4) % 4) * 2 + (yl + dy) % 2

    def cur_place(dz, dy, dc):
        return ((c + dc) % 2) * 8 + ((z + dz + 4) % 4) * 2 + (yh + dy) % 2

    mi = img_place(0, 0)
    mc = cur_place(0, 0, 0)
    for q, (dz, dy) in enumerate(PLACES):
        m = CM[q]
        high = jnp.max(m, axis=0, keepdims=True)
        lse = high + jnp.log(jnp.sum(CL[q] * jnp.exp(m - high), axis=0, keepdims=True))
        cst[mc, pl.ds(cur_place(dz, dy, 0), 1), :] = lse[:, :128]
        cst[mc, pl.ds(cur_place(dz, dy, 1), 1), :] = lse[:, 128:]
    for d in cur_peers:
        go(cst.at[mc], cst.at[mc], cur_dev(*d), 2, 16)
    for a, (dx, dy) in enumerate(PLACES):
        m = RM[a].T
        high = jnp.max(m, axis=0, keepdims=True)
        lse = high + jnp.log(jnp.sum(RL[a].T * jnp.exp(m - high), axis=0, keepdims=True))
        rst[mi, pl.ds(img_place(dx, dy), 1), :] = lse
    rst[mi, 8:16, :] = jnp.broadcast_to(pos, (8, 128))
    for d in img_peers:
        go(rst.at[mi], rst.at[mi], img_dev(*d), 3, 17)
    got(17, rst.at[0:7])
    parts = [rst[k, 0:8, :] for k in range(8)]
    high = functools.reduce(jnp.maximum, parts)
    tot_r[...] = high + jnp.log(functools.reduce(jnp.add, [jnp.exp(v - high) for v in parts]))
    for a, (dx, dy) in enumerate(PLACES):
        RM[a] = jnp.broadcast_to(tot_r[pl.ds(img_place(dx, dy), 1), :], (128, 128)).T
    got(16, cst.at[0:15])
    parts = [cst[k] for k in range(16)]
    high = functools.reduce(jnp.maximum, parts)
    tot_c[...] = high + jnp.log(functools.reduce(jnp.add, [jnp.exp(v - high) for v in parts]))

    for q, (dz, dy) in enumerate(PLACES):
        for h in range(2):
            CM[q, :, h * 128 : h * 128 + 128] = jnp.broadcast_to(tot_c[pl.ds(cur_place(dz, dy, h), 1), :], (8, 128))

    def weigh(q, a):
        rl = RM[a]
        for h in range(2):
            lanes = slice(h * 128, h * 128 + 128)
            s = S[q, a, :, lanes]
            cl = CM[q, 0:1, lanes]
            W[q, a, :, lanes] = ((jnp.exp(s - rl) + jnp.exp(s - cl)) * 0.5).astype(BF16)

    def weights_by_row(rows, qs):
        def step(a, carry):
            for q in qs:
                weigh(q, a)
            return carry

        lax.fori_loop(rows[0], rows[1], step, 0)

    def weights_by_col(cols, rows):
        def step(q, carry):
            for a in rows:
                weigh(q, a)
            return carry

        lax.fori_loop(cols[0], cols[1], step, 0)

    R_SWAP = 18

    def curve_part(q):
        part = tn(W[q].reshape(1024, 256), I[...].reshape(1024, 1024))
        qo[q, 1] = part[128:256]
        go(qo.at[q, 1], qoin.at[q], cur_dev(0, 0, 1), 4, R_SWAP + q)
        qo[q, 0] = part[0:128]

    def joined(q):
        got(R_SWAP + q, qoin.at[q])
        return qo[q, 0] + qoin[q]

    def image_part(a1, a2):
        w = jnp.concatenate(
            [jnp.concatenate([W[q, a] for q in range(8)], axis=1) for a in (a1, a2)], axis=0
        )
        return nn(w, C[...].reshape(2048, 1024))

    class Side:
        def __init__(self, w, into, keep, far, own, last, base, send, to):
            self.w, self.into, self.keep, self.far, self.own, self.last = w, into, keep, far, own, last
            self.base, self.send, self.to = base, send, to

        def go(self, y, k, h, d, dy, recv):
            go(self.w.at[y, k, h], self.into.at[y, k, h], self.to(d, dy), self.send, self.base + recv)

        def across(self, part):
            self.w[1, 0] = part.astype(BF16)
            for h in range(2):
                self.go(1, 0, HALF[h], 0, 1, h)

        def straight(self, d, part):
            k = 1 if d == 1 else 2
            self.w[1, k] = part.astype(BF16)
            self.go(1, k, slice(0, 128), d, 0, 2)

        def two_steps(self):
            for d, h in ring:
                got(self.base + h, py.at[0, HALF[0]])
                self.w[0, 0, HALF[h]] = (self.far[HALF[h]] + self.into[1, 0, HALF[h]].astype(F32)).astype(BF16)
                self.go(0, 0, HALF[h], d, 0, 3 + h)

        def first_half(self, d, part):
            k, through = (1, 0) if d == 1 else (2, 1)
            rest = HALF[1 - through]
            self.w[0, k, rest] = part[rest].astype(BF16)
            self.go(0, k, rest, d, 0, 5)
            self.keep[k - 1] = part[HALF[through]]

        def second_half(self):
            for d, h in ring:
                k = 1 if d == 1 else 2
                got(self.base + 3 + h, py.at[0, HALF[0]])
                self.w[0, k, HALF[h]] = (self.keep[k - 1] + self.into[0, 0, HALF[h]].astype(F32)).astype(BF16)
                self.go(0, k, HALF[h], d, 0, 5)

        def finish_partner(self):
            got(self.base + 2, I.at[0:2])
            self.last[0] = (self.own[1] + self.into[1, 1].astype(F32) + self.into[1, 2].astype(F32)).astype(BF16)
            go(self.last.at[0], self.last.at[1], self.to(0, 1), self.send, self.base + 6)

        def finish_own(self, other):
            got(self.base + 5, I.at[0:2])
            self.own[0] = self.own[0] + self.into[0, 1].astype(F32) + self.into[0, 2].astype(F32) - other

        def result(self):
            got(self.base + 6, I.at[0])
            return (self.own[0] + self.last[1].astype(F32)) * gain

    img = Side(pw, pin, pf, pa, pown, py, 26, 5, img_dev)
    cur = Side(qw, qin, qf, qa, qown, qy, 33, 5, lambda d, dy: cur_dev(d, dy, 0))

    weights_by_row((0, 8), (7,))
    curve_part(SLOT[2, 1])
    weights_by_col((0, 7), (4, 7))
    part = image_part(SLOT[2, 1], SLOT[2, 0])
    img.across(part[0:128])
    pa[...] = part[128:256]
    cur.across(joined(SLOT[2, 1]))
    weights_by_row((0, 4), (5, 6))
    weights_by_row((5, 7), (5, 6))
    curve_part(SLOT[1, 1])
    curve_part(SLOT[-1, 1])
    weights_by_col((0, 5), (5, 6))
    part = image_part(SLOT[1, 1], SLOT[-1, 1])
    img.straight(1, part[0:128])
    img.straight(-1, part[128:256])
    cur.straight(1, joined(SLOT[1, 1]))
    cur.straight(-1, joined(SLOT[-1, 1]))
    def grand(v):
        return jnp.sum(jnp.sum(v, axis=1, keepdims=True), axis=0, keepdims=True)

    pos_all = functools.reduce(jnp.add, [rst[k, 8:16, :] for k in range(8)])
    val_c[mc] = grand(tot_r[...]) - 2.0 * pos_all
    val_r[mi] = jnp.broadcast_to(grand(tot_c[...]), (8, 128))
    for d in cur_peers:
        go(val_c.at[mc], val_c.at[mc], cur_dev(*d), 6, 40)
    for d in img_peers:
        go(val_r.at[mi], val_r.at[mi], img_dev(*d), 7, 41)

    weights_by_col((0, 5), (0, 1, 2, 3))
    curve_part(SLOT[2, 0])
    curve_part(SLOT[1, 0])
    curve_part(SLOT[-1, 0])
    part = image_part(SLOT[1, 0], SLOT[-1, 0])
    img.two_steps()
    qa[...] = joined(SLOT[2, 0])
    cur.two_steps()
    img.first_half(1, part[0:128])
    img.first_half(-1, part[128:256])
    cur.first_half(1, joined(SLOT[1, 0]))
    cur.first_half(-1, joined(SLOT[-1, 0]))
    curve_part(SLOT[0, 1])
    curve_part(SLOT[0, 0])
    part = image_part(SLOT[0, 1], SLOT[0, 0])
    pown[1] = part[0:128]
    pown[0] = part[128:256]
    qown[1] = joined(SLOT[0, 1])
    qown[0] = joined(SLOT[0, 0])
    img.finish_partner()
    cur.finish_partner()
    img.second_half()
    cur.second_half()

    img.finish_own(C[0, 0].astype(F32))
    cur.finish_own(I[0].astype(F32))
    got(40, val_c.at[0:15])
    got(41, val_r.at[0:7])
    total = sum(val_c[k] for k in range(16)) + sum(val_r[k] for k in range(8))
    loss_ref[...] = total[0:1, 0:1] / (2.0 * pairs)
    dimg_ref[...] = img.result()
    dcur_ref[...] = cur.result()
    left(0, S.at[0:4, 0:7])
    left(1, S.at[0:2])
    left(2, cst.at[0:15])
    left(3, rst.at[0:7])
    left(4, S.at[0:4])
    left(5, S.at[0:4, 0:7])
    left(6, val_c.at[0:15])
    left(7, val_r.at[0:7])


def solution(mesh):
    def step(image_emb, curve_emb):
        gain = math.sqrt(image_emb.shape[1])
        vmem = pl.BlockSpec(memory_space=pltpu.VMEM)
        loss, dimg, dcur = pl.pallas_call(
            functools.partial(kernel, gain, 16384),
            out_shape=(
                jax.ShapeDtypeStruct((1, 1), F32),
                jax.ShapeDtypeStruct((128, 1024), F32),
                jax.ShapeDtypeStruct((128, 1024), F32),
            ),
            in_specs=[pl.BlockSpec(memory_space=pltpu.HBM)] * 2,
            out_specs=(vmem, vmem, vmem),
            scratch_shapes=[
                pltpu.VMEM((8, 128, 1024), BF16),
                pltpu.VMEM((8, 2, 128, 1024), BF16),
                pltpu.VMEM((8, 8, 128, 256), F32),
                pltpu.VMEM((8, 8, 128, 256), BF16),
                pltpu.VMEM((8, 128, 128), F32),
                pltpu.VMEM((8, 128, 128), F32),
                pltpu.VMEM((8, 8, 256), F32),
                pltpu.VMEM((8, 8, 256), F32),
                pltpu.VMEM((8, 16, 128), F32),
                pltpu.VMEM((16, 16, 128), F32),
                pltpu.VMEM((8, 128), F32),
                pltpu.VMEM((16, 128), F32),
                pltpu.VMEM((8, 8, 128), F32),
                pltpu.VMEM((16, 8, 128), F32),
                pltpu.VMEM((2, 3, 128, 1024), BF16),
                pltpu.VMEM((2, 3, 128, 1024), BF16),
                pltpu.VMEM((2, 64, 1024), F32),
                pltpu.VMEM((128, 1024), F32),
                pltpu.VMEM((2, 128, 1024), F32),
                pltpu.VMEM((2, 128, 1024), BF16),
                pltpu.VMEM((8, 2, 128, 1024), F32),
                pltpu.VMEM((8, 128, 1024), F32),
                pltpu.VMEM((2, 3, 128, 1024), BF16),
                pltpu.VMEM((2, 3, 128, 1024), BF16),
                pltpu.VMEM((2, 64, 1024), F32),
                pltpu.VMEM((128, 1024), F32),
                pltpu.VMEM((2, 128, 1024), F32),
                pltpu.VMEM((2, 128, 1024), BF16),
                pltpu.SemaphoreType.DMA((8,)),
                pltpu.SemaphoreType.DMA((42,)),
                pltpu.SemaphoreType.DMA((2,)),
            ],
            compiler_params=pltpu.CompilerParams(
                collective_id=0, has_side_effects=True, vmem_limit_bytes=57 << 20
            ),
        )(image_emb, curve_emb)
        return loss.reshape(()), dimg, dcur

    spec = P(("blk", "rep"), None)
    return jax.shard_map(step, mesh=mesh, in_specs=(spec, spec), out_specs=(P(), spec, spec), check_vma=False)
```

```python
import functools
import math

import jax
import jax.numpy as jnp
from jax import lax
from jax.experimental import pallas as pl
from jax.experimental.pallas import tpu as pltpu
from jax.sharding import PartitionSpec as P

F32, BF16 = jnp.float32, jnp.bfloat16
MESH = pl.DeviceIdType.MESH
PLACES = ((0, 0), (0, 1), (-1, 0), (1, 0), (2, 0), (-1, 1), (1, 1), (2, 1))
SLOT = {p: k for k, p in enumerate(PLACES)}
HALF = (slice(0, 64), slice(64, 128))


def nt(a, b):
    return lax.dot_general(a, b, (((1,), (1,)), ((), ())), preferred_element_type=F32)


def nn(a, b):
    return lax.dot_general(a, b, (((1,), (0,)), ((), ())), preferred_element_type=F32)


def tn(a, b):
    return lax.dot_general(a, b, (((0,), (0,)), ((), ())), preferred_element_type=F32)


def kernel(
    gain,
    pairs,
    img_ref,
    cur_ref,
    loss_ref,
    dimg_ref,
    dcur_ref,
    I,
    C,
    S,
    W,
    RM,
    RL,
    CM,
    CL,
    rst,
    cst,
    tot_r,
    tot_c,
    val_r,
    val_c,
    pw,
    pin,
    pf,
    pa,
    pown,
    py,
    qo,
    qoin,
    qw,
    qin,
    qf,
    qa,
    qown,
    qy,
    sends,
    recvs,
    locals_,
):
    blk, rep = lax.axis_index("blk"), lax.axis_index("rep")
    x = blk % 4
    z = (blk // 4) % 4
    yh = blk // 16
    yl = rep // 2
    c = rep % 2

    def dev(x, yl, z, yh, c):
        return ((yh * 4 + z) * 4 + x, yl * 2 + c)

    def img_dev(dx, dy):
        return dev((x + dx + 4) % 4, (yl + dy) % 2, z, yh, c)

    def cur_dev(dz, dy, dc):
        return dev(x, (yl + dy) % 2, (z + dz + 4) % 4, (yh + dy) % 2, (c + dc) % 2)

    def go(src, dst, device, send, recv):
        pltpu.make_async_remote_copy(
            src_ref=src,
            dst_ref=dst,
            send_sem=sends.at[send],
            recv_sem=recvs.at[recv],
            device_id=device,
            device_id_type=MESH,
        ).start()

    def got(recv, size):
        pltpu.make_async_copy(size, size, recvs.at[recv]).wait()

    def left(send, size):
        pltpu.make_async_copy(size, size, sends.at[send]).wait()

    load_i = pltpu.make_async_copy(img_ref, I.at[0], locals_.at[0])
    load_c = pltpu.make_async_copy(cur_ref, C.at[0, 0], locals_.at[1])
    load_i.start()
    load_c.start()

    img_peers = [(dx, dy) for dx in range(4) for dy in range(2) if dx or dy]
    cur_peers = [(dz, dy, dc) for dz in range(4) for dy in range(2) for dc in range(2) if dz or dy or dc]

    barrier = pltpu.get_barrier_semaphore()
    near = [img_dev(0, 1), img_dev(1, 0), img_dev(-1, 0)]
    near += [cur_dev(0, 1, 0), cur_dev(1, 0, 0), cur_dev(-1, 0, 0), cur_dev(0, 0, 1)]
    for d in near:
        pl.semaphore_signal(barrier, inc=1, device_id=d, device_id_type=MESH)
    load_i.wait()
    load_c.wait()
    pl.semaphore_wait(barrier, len(near))

    ring = ((1, 0), (-1, 1))
    back = ((1, 1), (-1, 0))
    G_Y, G_OWN, G_FAR, G_P, G_LAST, G_CORE = 0, 2, 6, 8, 10, 12

    def core(slot, h, group):
        go(C.at[slot, 0, HALF[h]], C.at[slot, 1, HALF[h]], cur_dev(0, 0, 1), 1, G_CORE + group)

    def both(i_src, c_src, slot, h, d, y, recv):
        go(i_src, I.at[slot, HALF[h]], img_dev(d, y), 0, recv)
        go(c_src, C.at[slot, 0, HALF[h]], cur_dev(d, y, 0), 0, recv)

    def onward(slot, to, h, d, y, recv):
        both(I.at[slot, HALF[h]], C.at[slot, 0, HALF[h]], to, h, d, y, recv)

    def own_sem(d, h):
        return G_OWN + (d + 1) + h

    for h in range(2):
        both(I.at[0, HALF[h]], C.at[0, 0, HALF[h]], 1, h, 0, 1, G_Y + h)
        for d, k in ring if h == 0 else back:
            both(I.at[0, HALF[k]], C.at[0, 0, HALF[k]], SLOT[-d, 0], k, d, 0, own_sem(d, k))
    go(C.at[0, 0], C.at[0, 1], cur_dev(0, 0, 1), 1, G_CORE)
    pos = jnp.sum(I[0].astype(F32) * C[0, 0].astype(F32), axis=1, keepdims=True) * gain
    pos = jnp.sum(pos, axis=0, keepdims=True)
    for d, h in ring:
        got(own_sem(d, h), I.at[0])
        onward(SLOT[-d, 0], SLOT[2, 0], h, d, 0, G_FAR + h)
        core(SLOT[-d, 0], h, 0)
    for h in range(2):
        got(G_Y + h, I.at[0])
        for d, k in ring if h == 0 else back:
            onward(1, SLOT[-d, 1], h, d, 0, G_P + h)
        core(1, h, 0)
        if h == 0:
            for d, k in back:
                got(own_sem(d, k), I.at[0])
                core(SLOT[-d, 0], k, 0)

    def scores(rows, cols):
        r0, r1 = rows

        def some(q, n):
            a = I[r0:r1].reshape((r1 - r0) * 128, 1024)
            s = nt(a, C[pl.ds(q, n)].reshape(n * 256, 1024)) * gain
            for k in range(n):
                S[q + k, r0:r1] = s[:, k * 256 : k * 256 + 256].reshape(r1 - r0, 128, 256)

        for q in range(cols[0], cols[1], 4):
            some(q, min(4, cols[1] - q))

    def row_stats(rows, cols, fresh):
        def step(a, carry):
            parts = [S[q, a, :, h * 128 : h * 128 + 128] for q in range(*cols) for h in range(2)]
            m = functools.reduce(jnp.maximum, parts)
            if fresh:
                total = functools.reduce(jnp.add, [jnp.exp(v - m) for v in parts])
            else:
                old = RM[a]
                m = jnp.maximum(m, old)
                total = RL[a] * jnp.exp(old - m)
                total = functools.reduce(jnp.add, [jnp.exp(v - m) for v in parts], total)
            RM[a] = m
            RL[a] = total
            return carry

        lax.fori_loop(rows[0], rows[1], step, 0)

    def col_stats(rows, cols, fresh):
        r0, r1 = rows

        def step(q, carry):
            s = S[q, r0:r1].reshape((r1 - r0) * 16, 8, 256)
            m = jnp.max(s, axis=0)
            if not fresh:
                old = CM[q]
                m = jnp.maximum(m, old)
            total = jnp.sum(jnp.exp(s - m[None]), axis=0)
            if not fresh:
                total = total + CL[q] * jnp.exp(old - m)
            CM[q] = m
            CL[q] = total
            return carry

        lax.fori_loop(cols[0], cols[1], step, 0)

    for h in range(2):
        got(G_FAR + h, I.at[0])
        onward(SLOT[2, 0], SLOT[2, 1], h, 0, 1, G_LAST + h)
        core(SLOT[2, 0], h, 1)
    got(G_CORE, S.at[0])
    scores((0, 4), (0, 4))
    row_stats((0, 4), (0, 4), True)
    col_stats((0, 4), (0, 4), True)
    got(G_CORE + 1, I.at[0])
    scores((4, 5), (0, 4))
    scores((0, 5), (4, 5))
    for h in range(2):
        got(G_P + h, I.at[0:2])
        core(SLOT[1, 1], h, 2)
        core(SLOT[-1, 1], h, 2)
    got(G_CORE + 2, I.at[0:2])
    scores((5, 7), (0, 5))
    scores((0, 7), (5, 7))
    row_stats((0, 4), (4, 7), False)
    row_stats((4, 7), (0, 7), True)
    col_stats((4, 7), (0, 4), False)
    col_stats((0, 7), (4, 7), True)
    for h in range(2):
        got(G_LAST + h, I.at[0])
        core(SLOT[2, 1], h, 3)
    scores((7, 8), (0, 7))
    got(G_CORE + 3, I.at[0])
    scores((0, 8), (7, 8))
    col_stats((7, 8), (0, 7), False)
    col_stats((0, 8), (7, 8), True)
    row_stats((0, 7), (7, 8), False)
    row_stats((7, 8), (0, 8), True)

    def img_place(dx, dy):
        return ((x + dx + 4) % 4) * 2 + (yl + dy) % 2

    def cur_place(dz, dy, dc):
        return ((c + dc) % 2) * 8 + ((z + dz + 4) % 4) * 2 + (yh + dy) % 2

    mi = img_place(0, 0)
    mc = cur_place(0, 0, 0)
    for q, (dz, dy) in enumerate(PLACES):
        m = CM[q]
        high = jnp.max(m, axis=0, keepdims=True)
        lse = high + jnp.log(jnp.sum(CL[q] * jnp.exp(m - high), axis=0, keepdims=True))
        cst[mc, pl.ds(cur_place(dz, dy, 0), 1), :] = lse[:, :128]
        cst[mc, pl.ds(cur_place(dz, dy, 1), 1), :] = lse[:, 128:]
    for d in cur_peers:
        go(cst.at[mc], cst.at[mc], cur_dev(*d), 2, 16)
    for a, (dx, dy) in enumerate(PLACES):
        m = RM[a].T
        high = jnp.max(m, axis=0, keepdims=True)
        lse = high + jnp.log(jnp.sum(RL[a].T * jnp.exp(m - high), axis=0, keepdims=True))
        rst[mi, pl.ds(img_place(dx, dy), 1), :] = lse
    rst[mi, 8:16, :] = jnp.broadcast_to(pos, (8, 128))
    for d in img_peers:
        go(rst.at[mi], rst.at[mi], img_dev(*d), 3, 17)
    got(17, rst.at[0:7])
    parts = [rst[k, 0:8, :] for k in range(8)]
    high = functools.reduce(jnp.maximum, parts)
    tot_r[...] = high + jnp.log(functools.reduce(jnp.add, [jnp.exp(v - high) for v in parts]))
    for a, (dx, dy) in enumerate(PLACES):
        RM[a] = jnp.broadcast_to(tot_r[pl.ds(img_place(dx, dy), 1), :] + math.log(2.0), (128, 128)).T
    got(16, cst.at[0:15])
    parts = [cst[k] for k in range(16)]
    high = functools.reduce(jnp.maximum, parts)
    tot_c[...] = high + jnp.log(functools.reduce(jnp.add, [jnp.exp(v - high) for v in parts]))

    for q, (dz, dy) in enumerate(PLACES):
        for h in range(2):
            CM[q, :, h * 128 : h * 128 + 128] = jnp.broadcast_to(tot_c[pl.ds(cur_place(dz, dy, h), 1), :] + math.log(2.0), (8, 128))

    def weigh(q, a):
        rl = RM[a]
        for h in range(2):
            lanes = slice(h * 128, h * 128 + 128)
            s = S[q, a, :, lanes]
            cl = CM[q, 0:1, lanes]
            W[q, a, :, lanes] = (jnp.exp(s - rl) + jnp.exp(s - cl)).astype(BF16)

    def weights_by_row(rows, qs):
        def step(a, carry):
            for q in qs:
                weigh(q, a)
            return carry

        lax.fori_loop(rows[0], rows[1], step, 0)

    def weights_by_col(cols, rows):
        def step(q, carry):
            for a in rows:
                weigh(q, a)
            return carry

        lax.fori_loop(cols[0], cols[1], step, 0)

    R_SWAP = 18

    def curve_part(q):
        part = tn(W[q].reshape(1024, 256), I[...].reshape(1024, 1024))
        qo[q, 1] = part[128:256]
        go(qo.at[q, 1], qoin.at[q], cur_dev(0, 0, 1), 4, R_SWAP + q)
        qo[q, 0] = part[0:128]

    def joined(q):
        got(R_SWAP + q, qoin.at[q])
        return qo[q, 0] + qoin[q]

    def image_part(a1, a2):
        w = jnp.concatenate(
            [jnp.concatenate([W[q, a] for q in range(8)], axis=1) for a in (a1, a2)], axis=0
        )
        return nn(w, C[...].reshape(2048, 1024))

    class Side:
        def __init__(self, w, into, keep, far, own, last, base, send, to):
            self.w, self.into, self.keep, self.far, self.own, self.last = w, into, keep, far, own, last
            self.base, self.send, self.to = base, send, to

        def go(self, y, k, h, d, dy, recv):
            go(self.w.at[y, k, h], self.into.at[y, k, h], self.to(d, dy), self.send, self.base + recv)

        def across(self, part):
            self.w[1, 0] = part.astype(BF16)
            for h in range(2):
                self.go(1, 0, HALF[h], 0, 1, h)

        def straight(self, d, part):
            k = 1 if d == 1 else 2
            self.w[1, k] = part.astype(BF16)
            self.go(1, k, slice(0, 128), d, 0, 2)

        def two_steps(self):
            for d, h in ring:
                got(self.base + h, py.at[0, HALF[0]])
                self.w[0, 0, HALF[h]] = (self.far[HALF[h]] + self.into[1, 0, HALF[h]].astype(F32)).astype(BF16)
                self.go(0, 0, HALF[h], d, 0, 3 + h)

        def first_half(self, d, part):
            k, through = (1, 0) if d == 1 else (2, 1)
            rest = HALF[1 - through]
            self.w[0, k, rest] = part[rest].astype(BF16)
            self.go(0, k, rest, d, 0, 5)
            self.keep[k - 1] = part[HALF[through]]

        def second_half(self):
            for d, h in ring:
                k = 1 if d == 1 else 2
                got(self.base + 3 + h, py.at[0, HALF[0]])
                self.w[0, k, HALF[h]] = (self.keep[k - 1] + self.into[0, 0, HALF[h]].astype(F32)).astype(BF16)
                self.go(0, k, HALF[h], d, 0, 5)

        def finish_partner(self):
            got(self.base + 2, I.at[0:2])
            self.last[0] = (self.own[1] + self.into[1, 1].astype(F32) + self.into[1, 2].astype(F32)).astype(BF16)
            go(self.last.at[0], self.last.at[1], self.to(0, 1), self.send, self.base + 6)

        def finish_own(self, other):
            got(self.base + 5, I.at[0:2])
            self.own[0] = self.own[0] + self.into[0, 1].astype(F32) + self.into[0, 2].astype(F32) - other

        def result(self):
            got(self.base + 6, I.at[0])
            return (self.own[0] + self.last[1].astype(F32)) * gain

    img = Side(pw, pin, pf, pa, pown, py, 26, 5, img_dev)
    cur = Side(qw, qin, qf, qa, qown, qy, 33, 5, lambda d, dy: cur_dev(d, dy, 0))

    weights_by_row((0, 8), (7,))
    curve_part(SLOT[2, 1])
    weights_by_col((0, 7), (4, 7))
    part = image_part(SLOT[2, 1], SLOT[2, 0])
    img.across(part[0:128])
    pa[...] = part[128:256]
    cur.across(joined(SLOT[2, 1]))
    weights_by_row((0, 4), (5, 6))
    weights_by_row((5, 7), (5, 6))
    curve_part(SLOT[1, 1])
    curve_part(SLOT[-1, 1])
    weights_by_col((0, 5), (5, 6))
    part = image_part(SLOT[1, 1], SLOT[-1, 1])
    img.straight(1, part[0:128])
    img.straight(-1, part[128:256])
    cur.straight(1, joined(SLOT[1, 1]))
    cur.straight(-1, joined(SLOT[-1, 1]))
    def grand(v):
        return jnp.sum(jnp.sum(v, axis=1, keepdims=True), axis=0, keepdims=True)

    pos_all = functools.reduce(jnp.add, [rst[k, 8:16, :] for k in range(8)])
    val_c[mc] = grand(tot_r[...]) - 2.0 * pos_all
    val_r[mi] = jnp.broadcast_to(grand(tot_c[...]), (8, 128))
    for d in cur_peers:
        go(val_c.at[mc], val_c.at[mc], cur_dev(*d), 6, 40)
    for d in img_peers:
        go(val_r.at[mi], val_r.at[mi], img_dev(*d), 7, 41)

    weights_by_col((0, 5), (0, 1, 2, 3))
    curve_part(SLOT[2, 0])
    curve_part(SLOT[1, 0])
    curve_part(SLOT[-1, 0])
    part = image_part(SLOT[1, 0], SLOT[-1, 0])
    img.two_steps()
    qa[...] = joined(SLOT[2, 0])
    cur.two_steps()
    img.first_half(1, part[0:128])
    img.first_half(-1, part[128:256])
    cur.first_half(1, joined(SLOT[1, 0]))
    cur.first_half(-1, joined(SLOT[-1, 0]))
    curve_part(SLOT[0, 1])
    curve_part(SLOT[0, 0])
    part = image_part(SLOT[0, 1], SLOT[0, 0])
    pown[1] = part[0:128]
    pown[0] = part[128:256]
    qown[1] = joined(SLOT[0, 1])
    qown[0] = joined(SLOT[0, 0])
    img.finish_partner()
    cur.finish_partner()
    img.second_half()
    cur.second_half()

    img.finish_own(C[0, 0].astype(F32))
    cur.finish_own(I[0].astype(F32))
    got(40, val_c.at[0:15])
    got(41, val_r.at[0:7])
    total = sum(val_c[k] for k in range(16)) + sum(val_r[k] for k in range(8))
    loss_ref[...] = total[0:1, 0:1] / (2.0 * pairs)
    dimg_ref[...] = img.result()
    dcur_ref[...] = cur.result()
    left(0, S.at[0:4, 0:7])
    left(1, S.at[0:2])
    left(2, cst.at[0:15])
    left(3, rst.at[0:7])
    left(4, S.at[0:4])
    left(5, S.at[0:4, 0:7])
    left(6, val_c.at[0:15])
    left(7, val_r.at[0:7])


def solution(mesh):
    def step(image_emb, curve_emb):
        gain = math.sqrt(image_emb.shape[1])
        vmem = pl.BlockSpec(memory_space=pltpu.VMEM)
        loss, dimg, dcur = pl.pallas_call(
            functools.partial(kernel, gain, 16384),
            out_shape=(
                jax.ShapeDtypeStruct((1, 1), F32),
                jax.ShapeDtypeStruct((128, 1024), F32),
                jax.ShapeDtypeStruct((128, 1024), F32),
            ),
            in_specs=[pl.BlockSpec(memory_space=pltpu.HBM)] * 2,
            out_specs=(vmem, vmem, vmem),
            scratch_shapes=[
                pltpu.VMEM((8, 128, 1024), BF16),
                pltpu.VMEM((8, 2, 128, 1024), BF16),
                pltpu.VMEM((8, 8, 128, 256), F32),
                pltpu.VMEM((8, 8, 128, 256), BF16),
                pltpu.VMEM((8, 128, 128), F32),
                pltpu.VMEM((8, 128, 128), F32),
                pltpu.VMEM((8, 8, 256), F32),
                pltpu.VMEM((8, 8, 256), F32),
                pltpu.VMEM((8, 16, 128), F32),
                pltpu.VMEM((16, 16, 128), F32),
                pltpu.VMEM((8, 128), F32),
                pltpu.VMEM((16, 128), F32),
                pltpu.VMEM((8, 8, 128), F32),
                pltpu.VMEM((16, 8, 128), F32),
                pltpu.VMEM((2, 3, 128, 1024), BF16),
                pltpu.VMEM((2, 3, 128, 1024), BF16),
                pltpu.VMEM((2, 64, 1024), F32),
                pltpu.VMEM((128, 1024), F32),
                pltpu.VMEM((2, 128, 1024), F32),
                pltpu.VMEM((2, 128, 1024), BF16),
                pltpu.VMEM((8, 2, 128, 1024), F32),
                pltpu.VMEM((8, 128, 1024), F32),
                pltpu.VMEM((2, 3, 128, 1024), BF16),
                pltpu.VMEM((2, 3, 128, 1024), BF16),
                pltpu.VMEM((2, 64, 1024), F32),
                pltpu.VMEM((128, 1024), F32),
                pltpu.VMEM((2, 128, 1024), F32),
                pltpu.VMEM((2, 128, 1024), BF16),
                pltpu.SemaphoreType.DMA((8,)),
                pltpu.SemaphoreType.DMA((42,)),
                pltpu.SemaphoreType.DMA((2,)),
            ],
            compiler_params=pltpu.CompilerParams(
                collective_id=0, has_side_effects=True, vmem_limit_bytes=57 << 20
            ),
        )(image_emb, curve_emb)
        return loss.reshape(()), dimg, dcur

    spec = P(("blk", "rep"), None)
    return jax.shard_map(step, mesh=mesh, in_specs=(spec, spec), out_specs=(P(), spec, spec), check_vma=False)
```
